32 devices in a mesh: dp: 8 (over z, x), tensor: 4 (over y, core).
Axes of the slice: x: 2, y: 2, z: 4, core: 2. Of those that a mesh axis runs over, the one named last changes fastest.
Arguments:
- hidden_in: bfloat16 [8192, 768], P('dp'), may hold values from -6 to 6
- document_time_vectors: bfloat16 [8, 4, 768], P('dp'), may hold values from -3 to 3
- segment_ids: int32 [8, 1024], P('dp'), may hold values from 0 to 3, never falling along the last dimension, each value on 1 to 512 neighbouring positions
- first_gain: bfloat16 [768], replicated, may hold values from 0.5 to 1.5
- first_shift: bfloat16 [768], replicated, may hold values from -2 to 2
- query_weight: bfloat16 [768, 768], P(None, 'tensor'), may hold values from -0.21875 to 0.21875
- query_bias: bfloat16 [768], P('tensor'), may hold values from -2 to 2
- key_weight: bfloat16 [768, 768], P(None, 'tensor'), may hold values from -0.21875 to 0.21875
- value_weight: bfloat16 [768, 768], P(None, 'tensor'), may hold values from -0.21875 to 0.21875
- value_bias: bfloat16 [768], P('tensor'), may hold values from -2 to 2
- out_weight: bfloat16 [768, 768], P('tensor'), may hold values from -2.5 to 2.5
- out_bias: bfloat16 [768], replicated, may hold values from -2 to 2
- second_gain: bfloat16 [768], replicated, may hold values from 0.5 to 1.5
- second_shift: bfloat16 [768], replicated, may hold values from -2 to 2
- up_weight: bfloat16 [768, 3072], P(None, 'tensor'), may hold values from -0.21875 to 0.21875
- up_bias: bfloat16 [3072], P('tensor'), may hold values from -2 to 2
- down_weight: bfloat16 [3072, 768], P('tensor'), may hold values from -0.109375 to 0.109375
- down_bias: bfloat16 [768], replicated, may hold values from -2 to 2
- cotangent: bfloat16 [8192, 768], P('dp'), may hold values from -6 to 6
Outputs:
- layer_out: bfloat16 [8192, 768], P('dp')
- hidden_input_gradient: float32 [8192, 768], P('dp')
- embed_grad: float32 [8, 4, 768], P('dp')
- first_gain_grad: float32 [768], P('dp')
- first_shift_grad: float32 [768], P('dp')
- query_weight_grad: float32 [768, 768], P('dp', 'tensor')
- query_bias_grad: float32 [768], P(('tensor', 'dp'))
- key_weight_grad: float32 [768, 768], P('dp', 'tensor')
- value_weight_grad: float32 [768, 768], P('dp', 'tensor')
- value_bias_grad: float32 [768], P(('tensor', 'dp'))
- out_weight_grad: float32 [768, 768], P('tensor', 'dp')
- out_bias_grad: float32 [768], P('dp')
- second_gain_grad: float32 [768], P('dp')
- second_shift_grad: float32 [768], P('dp')
- up_weight_grad: float32 [768, 3072], P('dp', 'tensor')
- up_bias_grad: float32 [3072], P(('tensor', 'dp'))
- down_weight_grad: float32 [3072, 768], P('tensor', 'dp')
- down_bias_grad: float32 [768], P('dp')
The draws below stay inside these ranges and needn't reach their ends.
Inputs may be any that keep to these rules, and one draw needn't show every extreme that they name: `segment_ids`: within a sequence the document numbers never fall; each of the 4 documents holds 1 to 512 tokens, one exactly that many.
All inputs are finite; a program needn't handle non-finite values.
Results may differ from the reference program's by a relative error of at most 0.019.
Values may be sent and summed in bfloat16 or wider, within the bound.
A program may use at most 128 MiB of HBM per device.

```python
import math
import jax
import jax.numpy as jnp
import numpy as np
from jax import lax

MODEL_WIDTH = 768
NHEAD = 12
DH = 64
FF = 3072
LENGTH = 1024
DOCS = 4
SEQS = 8
TOKENS = 8192


def level_of(stream_key, shape, pieces, low, largest):
    def one(axis_at, parts):
        steps = jax.random.uniform(jax.random.fold_in(jax.random.fold_in(stream_key, 6), axis_at), (parts,), jnp.float32, low / len(pieces), largest / len(pieces))
        return jnp.repeat(jnp.exp(steps), shape[axis_at] // parts).reshape((-1,) + (1,) * (len(shape) - axis_at - 1))

    loudness = one(*pieces[0])
    for cut in pieces[1:]:
        loudness = loudness * one(*cut)
    return loudness


def profile(count, total, reach, skew):
    loads = [(1 << 20) // math.isqrt(standing ** skew) + 1 for standing in range(2, count + 1)]
    spare, holding = total - reach - (count - 1), [1] * (count - 1)
    while spare > 0:
        candidates = [i for i in range(count - 1) if holding[i] < reach]
        pool, remaining = sum([loads[i] for i in candidates]), spare
        for i in candidates:
            addition = min(reach - holding[i], max(1, remaining * loads[i] // pool), spare)
            holding[i] = holding[i] + addition
            spare = spare - addition
    return np.array([reach] + holding)


def uneven(stream_key, count, total, limit, skew):
    if count == 2:
        one = jax.random.randint(stream_key, (), max(1, total - limit), min(limit, total - 1) + 1)
        return jnp.stack([one, total - one])
    tallies = jnp.asarray(profile(count, total, limit, skew), jnp.int32)
    twos = (count - 1) // 2
    donor, sink = tallies[1:1 + 2 * twos:2], tallies[2:2 + 2 * twos:2]
    room = jnp.minimum(donor - 1, limit - sink)
    shifted = jax.random.randint(jax.random.fold_in(stream_key, 1), (twos,), 0, 1 << 20) % (room + 1)
    tallies = tallies.at[1:1 + 2 * twos:2].set(donor - shifted).at[2:2 + 2 * twos:2].set(sink + shifted)
    return tallies[jax.random.permutation(jax.random.fold_in(stream_key, 2), count)]


def centred(stream_key, extent, scale, reach, cuts=(), held_as=jnp.bfloat16):
    level = level_of(stream_key, extent, cuts, -0.22, 0.18) if cuts else 1.0
    values = jax.random.normal(stream_key, extent, jnp.float32) * scale * level
    return jnp.minimum(jnp.maximum(values, -reach), reach).astype(held_as)


def setup_inputs(seed: int = 0) -> dict:
    splits = jax.random.split(jax.random.key(seed), 20)
    return {
        "hidden_in": centred(splits[0], (TOKENS, MODEL_WIDTH), 1.0, 6.0, ((0, 8),)),
        "document_time_vectors": centred(splits[1], (SEQS, DOCS, MODEL_WIDTH), 0.5, 3.0, ((0, 8),)),
        "segment_ids": jax.vmap(lambda own: jnp.searchsorted(jnp.cumsum(uneven(own, DOCS, LENGTH, LENGTH // 2, 0)), jnp.arange(LENGTH), side="right"))(jax.random.split(splits[2], SEQS)).reshape((SEQS, LENGTH)).astype(jnp.int32),
        "first_gain": jnp.clip(1.0 + 0.1 * jax.random.normal(splits[3], (MODEL_WIDTH,), jnp.float32), 0.5, 1.5).astype(jnp.bfloat16),
        "first_shift": centred(splits[4], (MODEL_WIDTH,), 0.3, 2.0),
        "query_weight": centred(splits[5], (MODEL_WIDTH, MODEL_WIDTH), MODEL_WIDTH ** -0.5, 0.21875, ((1, 4),)),
        "query_bias": centred(splits[6], (MODEL_WIDTH,), 0.3, 2.0, ((0, 4),)),
        "key_weight": centred(splits[7], (MODEL_WIDTH, MODEL_WIDTH), MODEL_WIDTH ** -0.5, 0.21875, ((1, 4),)),
        "value_weight": centred(splits[8], (MODEL_WIDTH, MODEL_WIDTH), MODEL_WIDTH ** -0.5, 0.21875, ((1, 4),)),
        "value_bias": centred(splits[9], (MODEL_WIDTH,), 0.3, 2.0, ((0, 4),)),
        "out_weight": centred(splits[10], (MODEL_WIDTH, MODEL_WIDTH), (MODEL_WIDTH // 128) ** -0.5, 2.5, ((0, 4),)),
        "out_bias": centred(splits[11], (MODEL_WIDTH,), 0.3, 2.0),
        "second_gain": jnp.clip(1.0 + 0.1 * jax.random.normal(splits[12], (MODEL_WIDTH,), jnp.float32), 0.5, 1.5).astype(jnp.bfloat16),
        "second_shift": centred(splits[13], (MODEL_WIDTH,), 0.3, 2.0),
        "up_weight": centred(splits[14], (MODEL_WIDTH, FF), MODEL_WIDTH ** -0.5, 0.21875, ((1, 4),)),
        "up_bias": centred(splits[15], (FF,), 0.3, 2.0, ((0, 4),)),
        "down_weight": centred(splits[16], (FF, MODEL_WIDTH), FF ** -0.5, 0.109375, ((0, 4),)),
        "down_bias": centred(splits[17], (MODEL_WIDTH,), 0.3, 2.0),
        "cotangent": centred(splits[18], (TOKENS, MODEL_WIDTH), 1.0, 6.0, ((0, 8),)),
    }


EPSILON = 1e-05
MASKED = -1000000000.0
HIGHEST_ACCURACY = lax.Precision.HIGHEST

@jax.custom_vjp
def low(v):
    return lax.optimization_barrier(v.astype(jnp.bfloat16)).astype(jnp.float32)

@jax.custom_vjp
def low_back(v):
    return v

def low_keep(v):
    return (low(v), None)

def low_pass(kept, grad):
    return (grad,)

def back_keep(v):
    return (v, None)

def back_low(kept, grad):
    return (low(grad),)
low.defvjp(low_keep, low_pass)
low_back.defvjp(back_keep, back_low)

def layer_norm(inputs, gains, shifts):
    average = lax.optimization_barrier(jnp.mean(inputs, axis=-1, keepdims=True))
    centered = inputs - average
    variance = lax.optimization_barrier(jnp.mean(centered * centered, axis=-1, keepdims=True))
    return centered * lax.rsqrt(variance + EPSILON) * gains + shifts

def dense(left, right):
    return jnp.dot(left, right, precision=HIGHEST_ACCURACY, preferred_element_type=jnp.float32)

def attend_sequence(packed):
    query_rows, key_rows, value_rows, doc_ids = packed
    length_total = doc_ids.shape[0]
    query_heads = query_rows.reshape(length_total, NHEAD, DH)
    key_heads = key_rows.reshape(length_total, NHEAD, DH)
    value_heads = value_rows.reshape(length_total, NHEAD, DH)
    scores = jnp.einsum('qhd,khd->hqk', query_heads, key_heads, precision=HIGHEST_ACCURACY) * (1.0 / math.sqrt(DH))
    same_doc = doc_ids[:, None] == doc_ids[None, :]
    scores = low_back(jnp.where(same_doc[None], scores, MASKED))
    probs = low(jax.nn.softmax(scores, axis=-1))
    mixed = jnp.einsum('hqk,khd->qhd', probs, value_heads, precision=HIGHEST_ACCURACY)
    return mixed.reshape(length_total, NHEAD * DH)

def make_layer(segment_ids):
    sequence_list, length_total = segment_ids.shape
    document_indicator = (segment_ids[:, :, None] == jnp.arange(DOCS, dtype=jnp.int32)[None, None, :]).astype(jnp.float32)

    def layer(hidden, embedding_table, first_gain, first_shift, query_weight, query_bias, key_weight, value_weight, value_bias, out_weight, out_bias, second_gain, second_shift, up_weight, up_bias, down_weight, down_bias):
        positioned_rows = jnp.einsum('bqz,bzy->bqy', document_indicator, embedding_table, precision=HIGHEST_ACCURACY).reshape(sequence_list * length_total, MODEL_WIDTH)
        resid_in = hidden + positioned_rows
        attn_in = low(layer_norm(resid_in, first_gain, first_shift))
        queries = low(low_back(dense(attn_in, query_weight) + query_bias))
        keys = low(low_back(dense(attn_in, key_weight)))
        values = low(low_back(dense(attn_in, value_weight) + value_bias))
        packed = (queries.reshape(sequence_list, length_total, MODEL_WIDTH), keys.reshape(sequence_list, length_total, MODEL_WIDTH), values.reshape(sequence_list, length_total, MODEL_WIDTH), segment_ids)
        mixed = lax.map(jax.checkpoint(attend_sequence), packed).reshape(sequence_list * length_total, MODEL_WIDTH)
        mixed = low(low_back(mixed))
        middle = resid_in + low_back(dense(mixed, out_weight) + out_bias)
        mlp_in = low(layer_norm(middle, second_gain, second_shift))
        pre_gelu = low_back(dense(mlp_in, up_weight) + up_bias)
        activated = low(jax.nn.gelu(pre_gelu, approximate=False))
        return middle + low_back(dense(activated, down_weight) + down_bias)
    return layer

def reference(hidden_in, document_time_vectors, segment_ids, first_gain, first_shift, query_weight, query_bias, key_weight, value_weight, value_bias, out_weight, out_bias, second_gain, second_shift, up_weight, up_bias, down_weight, down_bias, cotangent):
    inputs = (hidden_in, document_time_vectors, first_gain, first_shift, query_weight, query_bias, key_weight, value_weight, value_bias, out_weight, out_bias, second_gain, second_shift, up_weight, up_bias, down_weight, down_bias)
    floats = tuple((item.astype(jnp.float32) for item in inputs))
    result, pullback = jax.vjp(make_layer(segment_ids), *floats)
    grads = pullback(cotangent.astype(jnp.float32))
    return (result.astype(jnp.bfloat16), grads[0], grads[1], grads[2], grads[3], grads[4], grads[5], grads[6], grads[7], grads[8], grads[9], grads[10], grads[11], grads[12], grads[13], grads[14], grads[15], grads[16])
```

```python
import functools
import math
import types

import jax
import jax.numpy as jnp
from jax import lax
from jax.experimental import pallas as pl
from jax.experimental.pallas import tpu as pltpu
from jax.sharding import PartitionSpec as P

DH = 64
EPSILON = 1e-05
MASKED = -1000000000.0
BF = jnp.bfloat16
F32 = jnp.float32
MESH = pl.DeviceIdType.MESH
VMEM_LIMIT = 67_000_000


def dot(left, right, left_dim=1, right_dim=0):
    return lax.dot_general(
        left, right, (((left_dim,), (right_dim,)), ((), ())), preferred_element_type=F32
    )


def normalize(rows):
    average = jnp.mean(rows, axis=-1, keepdims=True)
    centered = rows - average
    variance = jnp.mean(centered * centered, axis=-1, keepdims=True)
    scale = lax.rsqrt(variance + EPSILON)
    return centered * scale, scale


def norm_back(normal, scale, gain, grad):
    inner = grad * gain
    first = jnp.mean(inner, axis=-1, keepdims=True)
    second = jnp.mean(inner * normal, axis=-1, keepdims=True)
    return scale * (inner - first - normal * second)


def packed_source(slots, start, half, block):
    return (1 - block) * (slots + start) + block * (slots + jnp.where(slots >= start, half, 0))


def longest_start(segments, docs):
    half = segments.shape[1] // 2
    longest = jnp.zeros((1, 1), F32)
    for doc in range(docs):
        count = jnp.sum(jnp.where(segments == doc, 1.0, 0.0), axis=1, keepdims=True)
        longest = longest + jnp.where(count == half, float(doc), 0.0)
    before = jnp.where(segments.astype(F32) < longest, 1.0, 0.0)
    return jnp.sum(before, axis=1, keepdims=True).astype(jnp.int32)


class Shape:
    def __init__(self, length, width, head_cols, hidden, docs, dp, chunk):
        self.length, self.width, self.head_cols, self.hidden = length, width, head_cols, hidden
        self.docs, self.dp = docs, dp
        self.rows = length // 2
        self.short = 4 <= dp <= 8 and width // dp % 16 == 0
        blocks = dp if self.short else 8
        self.zs = blocks // 2
        self.share = width // blocks
        self.own_share = width // dp
        self.chunk = chunk
        self.chunks = self.rows // chunk
        self.heads = head_cols // DH


def layer_kernel(s, names, *refs):
    r = types.SimpleNamespace(**dict(zip(names, refs)))
    width, rows_all, cols, hidden = s.width, s.rows, s.head_cols, s.hidden
    zs, share, chunk = s.zs, s.share, s.chunk
    dp_at, tensor_at = lax.axis_index("dp"), lax.axis_index("tensor")
    core, side = lax.rem(tensor_at, 2), lax.div(tensor_at, 2)
    x_at, z_at = lax.rem(dp_at, 2), lax.div(dp_at, 2)
    sibling = (dp_at, side * 2 + 1 - core)
    peer = (dp_at, (1 - side) * 2 + core)
    across = (z_at * 2 + 1 - x_at, tensor_at)

    def along(step):
        return (lax.rem(z_at + step, zs) * 2 + x_at, tensor_at)

    def local(source, target, at):
        return pltpu.make_async_copy(source, target, r.local_sem.at[at])

    def remote(source, target, at, device):
        return pltpu.make_async_remote_copy(
            src_ref=source,
            dst_ref=target,
            send_sem=r.send_sem.at[at],
            recv_sem=r.recv_sem.at[at],
            device_id=device,
            device_id_type=MESH,
        )

    W_AT, X1, X2, X3, X4 = 0, 8, 16, 24, 32
    GM, GA, MX, MZ, AX, AZ, SV, OUT = 40, 44, 46, 56, 64, 70, 74, 80

    barrier = pltpu.get_barrier_semaphore()
    partners = [sibling, peer]
    if s.short:
        partners = partners + [across] + [along(step) for step in range(1, zs)]
    for partner in partners:
        pl.semaphore_signal(barrier, inc=1, device_id=partner, device_id_type=MESH)

    weights = [
        (r.query, r.wqkv.at[:, 0]),
        (r.key, r.wqkv.at[:, 1]),
        (r.value, r.wqkv.at[:, 2]),
        (r.out, r.wo),
        (r.up, r.wu),
        (r.down, r.wd),
    ]
    local_hidden = local(r.hidden, r.hid, 0)
    local_hidden.start()
    own_weights = [local(src, dst.at[0], 2 + i) for i, (src, dst) in enumerate(weights)]
    for copy in own_weights[:4]:
        copy.start()
    local_cot = local(r.cotangent, r.cot, 1)
    local_cot.start()
    for copy in own_weights[4:]:
        copy.start()
    small = r.small
    rows_of = (r.first_gain, r.first_shift, r.second_gain, r.second_shift, r.out_bias, r.down_bias)
    for row, ref in enumerate(rows_of + (None, None, r.up_bias, r.query_bias, r.value_bias)):
        if ref is not None:
            n = ref.shape[0]
            small[row : row + 1, 0:n] = ref[...].reshape(1, n).astype(F32)
    pl.semaphore_wait(barrier, len(partners))
    small_copy = remote(r.small.at[pl.ds(8, 8)], r.small_sib, W_AT + 6, sibling)
    small_copy.start()
    sib_weights = [remote(src, dst.at[1], W_AT + i, sibling) for i, (src, dst) in enumerate(weights)]
    for copy in sib_weights:
        copy.start()

    gain_one, shift_one = small[0:1, :], small[1:2, :]
    gain_two, shift_two = small[2:3, :], small[3:4, :]
    out_bias, down_bias = small[4:5, :], small[5:6, :]
    start = longest_start(r.segments[...], s.docs)
    segments = r.segments[...]
    doc_lane = lax.broadcasted_iota(jnp.int32, (8, s.length), 0)
    docs_full = jnp.where(segments == doc_lane, 1.0, 0.0).astype(BF)
    doc_vectors = r.doc_vectors[0]

    def at(k):
        return pl.ds(pl.multiple_of(k * chunk, chunk), chunk)

    local_hidden.wait()
    for copy in own_weights[:3]:
        copy.wait()
    local_cot.wait()

    def projections(half, rows, source):
        for j in range(3):
            y = dot(source, r.wqkv[half, j], 1, 1)
            if j != 1:
                bias_row = small if half == 0 else r.small_sib
                base = 8 if half == 0 else 0
                y = y + bias_row[base + 1 + j // 2 : base + 2 + j // 2, 0:cols]
            r.qkv[half, j, rows, :] = y.astype(BF)

    def pack(k, _):
        rows = at(k)
        slots = lax.broadcasted_iota(jnp.int32, (chunk, 1), 0) + k * chunk
        source = packed_source(slots, start, rows_all, core)
        columns = lax.broadcasted_iota(jnp.int32, (chunk, s.length), 1)
        choose = jnp.where(columns == source, 1.0, 0.0).astype(BF)
        docs_here = dot(choose, docs_full, 1, 1).astype(BF)
        r.docs[rows, :] = docs_here
        x = dot(choose, r.hid[...]) + dot(docs_here[:, 0 : s.docs], doc_vectors)
        r.resid[rows, :] = x
        r.cotp[rows, :] = dot(choose, r.cot[...]).astype(BF)
        normal, _ = normalize(x)
        y = (normal * gain_one + shift_one).astype(BF)
        r.attn_in[rows, :] = y
        projections(0, rows, y)
        return 0

    lax.fori_loop(0, s.chunks, pack, 0)
    docs_all = r.docs[...]

    small_copy.wait_recv()
    for copy in sib_weights[:3]:
        copy.wait_recv()

    def second_half(k, _):
        rows = at(k)
        r.bias[rows, :] = (dot(r.docs[rows, :], docs_all, 1, 1) - 1.0) * (-MASKED)
        projections(1, rows, r.attn_in[rows, :])
        return 0

    lax.fori_loop(0, s.chunks, second_half, 0)
    own_weights[3].wait()
    sib_weights[3].wait_recv()

    lane = lax.broadcasted_iota(jnp.int32, (1, 128), 1)
    low = jnp.where(lane < DH, 1.0, 0.0)
    high = 1.0 - low
    factor = 1.0 / math.sqrt(DH)
    groups = [(0, 128, (low, high)), (128, 192, (None,))]

    def masked(values, mask, scale=1.0):
        if mask is None:
            return values if scale == 1.0 else values * jnp.asarray(scale, BF)
        return values * (mask * scale).astype(BF)

    def forward(k, _):
        rows = at(k)
        bias = r.bias[rows, :]
        partial = jnp.zeros((chunk, width), F32)
        for half in range(2):
            for first, last, masks in groups:
                q = r.qkv[half, 0, rows, first:last]
                keys = r.qkv[half, 1, :, first:last]
                values = r.qkv[half, 2, :, first:last]
                mixed = None
                for j, mask in enumerate(masks):
                    head = half * s.heads + first // DH + j
                    scores = dot(masked(q, mask, factor), keys, 1, 1) + bias
                    top = jnp.max(scores, axis=1, keepdims=True)
                    e = jnp.exp(scores - top)
                    total = jnp.sum(e, axis=1, keepdims=True)
                    probs = (e * (1.0 / total)).astype(BF)
                    r.probs[head, rows, :] = probs
                    part = dot(probs, masked(values, mask))
                    mixed = part if mixed is None else mixed + part
                r.mixed32[half, rows, first:last] = mixed
                r.mixed[half, rows, first:last] = mixed.astype(BF)
            partial = partial + dot(r.mixed[half, rows, :], r.wo[half])
        r.x1s[rows, :] = partial.astype(BF)
        remote(r.x1s.at[rows], r.x1r.at[rows], X1 + k, peer).start()
        return 0

    lax.fori_loop(0, s.chunks, forward, 0)

    own_weights[4].wait()
    own_weights[5].wait()
    sib_weights[4].wait_recv()
    sib_weights[5].wait_recv()
    up_bias = (small[8:9, :], r.small_sib[0:1, :])
    zero_rows = jnp.zeros_like(r.sums[...])
    r.sums[...] = zero_rows

    def add_sum(row, values):
        n = values.shape[1]
        r.sums[row : row + 1, 0:n] = r.sums[row : row + 1, 0:n] + jnp.sum(values, axis=0, keepdims=True)

    def mlp(k, _):
        rows = at(k)
        remote(r.x1s.at[rows], r.x1r.at[rows], X1 + k, peer).wait_recv()
        middle = (
            r.resid[rows, :]
            + (r.x1s[rows, :].astype(F32) + r.x1r[rows, :].astype(F32))
            + out_bias
        )
        r.middle[rows, :] = middle
        normal, _ = normalize(middle)
        source = (normal * gain_two + shift_two).astype(BF)
        r.mlp_in[rows, :] = source
        grad_top = r.cotp[rows, :]
        add_sum(5, grad_top.astype(F32))
        grad_in = jnp.zeros((chunk, width), F32)
        for half in range(2):
            r.pre[...] = dot(source, r.wu[half]) + up_bias[half]
            r.dact[...] = dot(grad_top, r.wd[half], 1, 1)

            def gelu(i, _):
                part = pl.ds(pl.multiple_of(i * 16, 16), 16)
                v = r.pre[part, :]
                cdf = 0.5 * (1.0 + lax.erf(v * math.sqrt(0.5)))
                pdf = jnp.exp(-0.5 * v * v) * (1.0 / math.sqrt(2.0 * math.pi))
                where = pl.ds(pl.multiple_of(k * chunk + i * 16, 16), 16)
                r.act[half, where, :] = (v * cdf).astype(BF)
                r.gpre[half, where, :] = (r.dact[part, :] * (cdf + v * pdf)).astype(BF)
                return 0

            lax.fori_loop(0, chunk // 16, gelu, 0)
            grad_pre = r.gpre[half, rows, :]
            add_sum(6 + 2 * half, grad_pre.astype(F32))
            grad_in = grad_in + dot(grad_pre, r.wu[half], 1, 1)
        r.x3s[rows, :] = grad_in.astype(BF)
        remote(r.x3s.at[rows], r.x3r.at[rows], X3 + k, peer).start()
        return 0

    lax.fori_loop(0, s.chunks, mlp, 0)

    def mlp_out(k, _):
        rows = at(k)
        part = dot(r.act[0, rows, :], r.wd[0]) + dot(r.act[1, rows, :], r.wd[1])
        r.x2s[rows, :] = part.astype(BF)
        remote(r.x2s.at[rows], r.x2r.at[rows], X2 + k, peer).start()
        return 0

    lax.fori_loop(0, s.chunks, mlp_out, 0)

    zh = zs // 2
    r.t1[...] = r.mlp_in[...].T
    r.t2[...] = r.cotp[...].T

    def mlp_grads(half, target):
        for kind, (left, right) in enumerate(((r.t1, r.gpre), (r.t2, r.act))):
            for part in range(2):
                top = part * zh * 2 * share
                y = dot(left[top : top + zh * 2 * share, :], right[half])
                target[part * zh : (part + 1) * zh, :, kind] = y.astype(BF).reshape(zh, 2, share, hidden)

    mlp_grads(1, r.gms)
    gm_copies = [
        remote(r.gms.at[:, :, kind], r.gmr.at[:, :, kind], GM + kind, sibling) for kind in range(2)
    ]
    for copy in gm_copies:
        copy.start()
    mlp_grads(0, r.gmo)
    for copy in gm_copies:
        copy.wait_recv()

    def x_sum(own, received, z, which):
        return own[z, which].astype(F32) + received[z, which].astype(F32)

    def x_stage(own, received, sent, landed, sem):
        for step in range(zs):
            z = lax.rem(z_at + 1 + step, zs)
            sent[z] = x_sum(own, received, z, 1 - x_at).astype(BF)
            remote(sent.at[z], landed.at[z], sem + step, across).start()

    def z_stage(own, received, sent, landed, total, x_sent, x_landed, x_sem, sem):
        for step in range(zs):
            z = lax.rem(z_at + 1 + step, zs)
            remote(x_sent.at[z], x_landed.at[z], x_sem + step, across).wait_recv()
            y = x_sum(own, received, z, x_at) + x_landed[z].astype(F32)
            if step == zs - 1:
                total[...] = y
            else:
                sent[step] = y.astype(BF)
                remote(sent.at[step], landed.at[step], sem + step, along(step + 1)).start()

    def last_stage(sent, landed, total, sem):
        y = total[...]
        for step in range(zs - 1):
            remote(sent.at[step], landed.at[step], sem + step, along(step + 1)).wait_recv()
            y = y + landed[step].astype(F32)
        total[...] = y

    def whole_sum(own, received, target):
        def add(z, _):
            target[z] = (own[z].astype(F32) + received[z].astype(F32)).astype(target_type)
            return 0

        target_type = target.dtype
        lax.fori_loop(0, zs, add, 0)

    if s.short:
        x_stage(r.gmo, r.gmr, r.mxs, r.mxr, MX)
    else:
        whole_sum(r.gmo, r.gmr, r.grad_mlp)

    r.dk[...] = jnp.zeros_like(r.dk[...])
    r.dv[...] = jnp.zeros_like(r.dv[...])

    def backward(k, _):
        rows = at(k)
        remote(r.x3s.at[rows], r.x3r.at[rows], X3 + k, peer).wait_recv()
        grad_in = r.x3s[rows, :].astype(F32) + r.x3r[rows, :].astype(F32)
        normal, scale = normalize(r.middle[rows, :])
        add_sum(2, grad_in * normal)
        add_sum(3, grad_in)
        grad_middle = r.cotp[rows, :].astype(F32) + norm_back(normal, scale, gain_two, grad_in)
        r.gmid[rows, :] = grad_middle
        grad_low = grad_middle.astype(BF)
        r.gml[rows, :] = grad_low
        add_sum(4, grad_low.astype(F32))
        for half in range(2):
            grad_mixed = dot(grad_low, r.wo[half], 1, 1).astype(BF)
            for first, last, masks in groups:
                q = r.qkv[half, 0, rows, first:last]
                keys = r.qkv[half, 1, :, first:last]
                values = r.qkv[half, 2, :, first:last]
                out = grad_mixed[:, first:last]
                product = out.astype(F32) * r.mixed32[half, rows, first:last]
                dq = dk = dv = None
                for j, mask in enumerate(masks):
                    head = half * s.heads + first // DH + j
                    inner = jnp.sum(product if mask is None else product * mask, axis=1, keepdims=True)
                    own_out = masked(out, mask)
                    probs = r.probs[head, rows, :]
                    grad_probs = dot(own_out, values, 1, 1)
                    grad_scores = (probs.astype(F32) * (grad_probs - inner)).astype(BF)
                    parts = (
                        dot(grad_scores, masked(keys, mask, factor)),
                        dot(grad_scores, masked(q, mask, factor), 0, 0),
                        dot(probs, own_out, 0, 0),
                    )
                    if dq is None:
                        dq, dk, dv = parts
                    else:
                        dq, dk, dv = dq + parts[0], dk + parts[1], dv + parts[2]
                r.dqkv[half, 0, rows, first:last] = dq.astype(BF)
                r.dk[half, :, first:last] = r.dk[half, :, first:last] + dk
                r.dv[half, :, first:last] = r.dv[half, :, first:last] + dv
        return 0

    lax.fori_loop(0, s.chunks, backward, 0)
    r.dqkv[:, 1] = r.dk[...].astype(BF)
    r.dqkv[:, 2] = r.dv[...].astype(BF)

    def attn_in_grad(k, _):
        rows = at(k)
        part = jnp.zeros((chunk, width), F32)
        for half in range(2):
            for j in range(3):
                part = part + dot(r.dqkv[half, j, rows, :], r.wqkv[half, j])
        r.x4s[rows, :] = part.astype(BF)
        remote(r.x4s.at[rows], r.x4r.at[rows], X4 + k, peer).start()
        return 0

    lax.fori_loop(0, s.chunks, attn_in_grad, 0)

    if s.short:
        z_stage(r.gmo, r.gmr, r.mzs, r.mzr, r.grad_mlp, r.mxs, r.mxr, MX, MZ)

    for half in range(2):
        add_sum(7 + 2 * half, r.dqkv[half, 0].astype(F32))
        add_sum(10 + half, r.dqkv[half, 2].astype(F32))
    r.t1[...] = r.attn_in[...].T
    r.t2[...] = r.gml[...].T

    def attn_grads(half, target):
        for kind in range(4):
            right = r.dqkv[half, kind] if kind < 3 else r.mixed[half]
            y = dot((r.t1 if kind < 3 else r.t2)[...], right)
            target[:, :, kind] = y.astype(BF).reshape(zs, 2, share, cols)

    attn_grads(1, r.gas)
    ga_copy = remote(r.gas, r.gar, GA, sibling)
    ga_copy.start()
    attn_grads(0, r.gao)
    ga_copy.wait_recv()
    if s.short:
        x_stage(r.gao, r.gar, r.axs, r.axr, AX)
    else:
        whole_sum(r.gao, r.gar, r.grad_attn)

    def output(k, _):
        rows = at(k)
        remote(r.x2s.at[rows], r.x2r.at[rows], X2 + k, peer).wait_recv()
        y = r.middle[rows, :] + (r.x2s[rows, :].astype(F32) + r.x2r[rows, :].astype(F32)) + down_bias
        r.lo[rows, :] = y.astype(BF)
        return 0

    lax.fori_loop(0, s.chunks, output, 0)
    lo_copy = remote(r.lo, r.layer_out.at[core], OUT, sibling)
    lo_copy.start()
    lo_local = local(r.lo, r.layer_out.at[core], 8)
    lo_local.start()

    if s.short:
        last_stage(r.mzs, r.mzr, r.grad_mlp, MZ)
        z_stage(r.gao, r.gar, r.azs, r.azr, r.grad_attn, r.axs, r.axr, AX, AZ)

    def input_grad(k, _):
        rows = at(k)
        remote(r.x4s.at[rows], r.x4r.at[rows], X4 + k, peer).wait_recv()
        grad_in = r.x4s[rows, :].astype(F32) + r.x4r[rows, :].astype(F32)
        normal, scale = normalize(r.resid[rows, :])
        add_sum(0, grad_in * normal)
        add_sum(1, grad_in)
        y = r.gmid[rows, :] + norm_back(normal, scale, gain_one, grad_in)
        r.ig[rows, :] = y.astype(BF)
        return 0

    lax.fori_loop(0, s.chunks, input_grad, 0)
    ig_copy = remote(r.ig, r.input_grad.at[core], OUT + 1, sibling)
    ig_copy.start()
    ig_local = local(r.ig, r.input_grad.at[core], 9)
    ig_local.start()
    sums_copy = remote(r.sums, r.sums_r, SV, sibling)
    sums_copy.start()

    if s.short:
        last_stage(r.azs, r.azr, r.grad_attn, AZ)
    sums_copy.wait_recv()
    mine, other = r.sums, r.sums_r
    r.vec[0:6, :] = mine[0:6, :] + other[0:6, :]
    r.vec[6:7, :] = mine[6:7, :] + other[8:9, :]
    r.vec[7:8, :] = jnp.zeros((1, width), F32)
    r.vec[7:8, 0:cols] = mine[7:8, 0:cols] + other[9:10, 0:cols]
    r.vec[7:8, 256 : 256 + cols] = mine[10:11, 0:cols] + other[11:12, 0:cols]
    sends = [small_copy, ga_copy, lo_copy, ig_copy, sums_copy] + sib_weights + gm_copies
    if s.short:
        vec_copy = remote(r.vec, r.vec_r, SV + 1, across)
        vec_copy.start()
        vec_copy.wait_recv()
        r.vec2[...] = r.vec[...] + r.vec_r[...]
        vec_z = [remote(r.vec2, r.vec_z.at[step], SV + 2 + step, along(step + 1)) for step in range(zs - 1)]
        for copy in vec_z:
            copy.start()
        total = r.vec2[...]
        for step, copy in enumerate(vec_z):
            copy.wait_recv()
            total = total + r.vec_z[step]
        r.vectors[...] = total
        sends = sends + [vec_copy] + vec_z
        for sent, landed, sem in ((r.mxs, r.mxr, MX), (r.axs, r.axr, AX)):
            for step in range(zs):
                z = lax.rem(z_at + 1 + step, zs)
                sends.append(remote(sent.at[z], landed.at[z], sem + step, across))
        for sent, landed, sem in ((r.mzs, r.mzr, MZ), (r.azs, r.azr, AZ)):
            for step in range(zs - 1):
                sends.append(remote(sent.at[step], landed.at[step], sem + step, along(step + 1)))
    else:
        r.vectors[...] = r.vec[...]

    for k in range(s.chunks):
        rows = pl.ds(k * chunk, chunk)
        for sent, landed, sem in ((r.x1s, r.x1r, X1), (r.x2s, r.x2r, X2), (r.x3s, r.x3r, X3), (r.x4s, r.x4r, X4)):
            remote(sent.at[rows], landed.at[rows], sem + k, peer).wait_send()
    for copy in sends:
        copy.wait_send()
    lo_copy.wait_recv()
    ig_copy.wait_recv()
    lo_local.wait()
    ig_local.wait()


def layer_call(s, vectors, arrays):
    n, width, cols, hid = s.rows, s.width, s.head_cols, s.hidden
    zs, share = s.zs, s.share
    outputs = dict(
        layer_out=((2, n, width), BF, pl.ANY),
        input_grad=((2, n, width), BF, pl.ANY),
        grad_mlp=((2, share, hid) if s.short else (zs, 2, 2, share, hid), F32 if s.short else BF, pltpu.VMEM),
        grad_attn=((4, share, cols) if s.short else (zs, 2, 4, share, cols), F32 if s.short else BF, pltpu.VMEM),
        vectors=((8, width), F32, pltpu.VMEM),
    )
    scratch = dict(
        hid=((s.length, width), BF),
        cot=((s.length, width), BF),
        wqkv=((2, 3, cols, width), BF),
        wo=((2, cols, width), BF),
        wu=((2, width, hid), BF),
        wd=((2, hid, width), BF),
        small=((16, width), F32),
        small_sib=((8, width), F32),
        docs=((n, 8), BF),
        bias=((n, n), F32),
        resid=((n, width), F32),
        attn_in=((n, width), BF),
        cotp=((n, width), BF),
        qkv=((2, 3, n, cols), BF),
        probs=((2 * s.heads, n, n), BF),
        mixed32=((2, n, cols), F32),
        mixed=((2, n, cols), BF),
        middle=((n, width), F32),
        mlp_in=((n, width), BF),
        act=((2, n, hid), BF),
        gpre=((2, n, hid), BF),
        pre=((s.chunk, hid), F32),
        dact=((s.chunk, hid), F32),
        gmid=((n, width), F32),
        gml=((n, width), BF),
        dk=((2, n, cols), F32),
        dv=((2, n, cols), F32),
        dqkv=((2, 3, n, cols), BF),
        t1=((width, n), BF),
        t2=((width, n), BF),
        gms=((zs, 2, 2, share, hid), BF),
        gmo=((zs, 2, 2, share, hid), BF),
        gmr=((zs, 2, 2, share, hid), BF),
        gas=((zs, 2, 4, share, cols), BF),
        gao=((zs, 2, 4, share, cols), BF),
        gar=((zs, 2, 4, share, cols), BF),
        sums=((16, width), F32),
        sums_r=((16, width), F32),
        vec=((8, width), F32),
    )
    if s.short:
        scratch.update(
                mxs=((zs, 2, share, hid), BF),
                mxr=((zs, 2, share, hid), BF),
                mzs=((zs - 1, 2, share, hid), BF),
                mzr=((zs - 1, 2, share, hid), BF),
                axs=((zs, 4, share, cols), BF),
                axr=((zs, 4, share, cols), BF),
                azs=((zs - 1, 4, share, cols), BF),
                azr=((zs - 1, 4, share, cols), BF),
                vec_r=((8, width), F32),
                vec2=((8, width), F32),
                vec_z=((zs - 1, 8, width), F32),
        )
    swap = ((n, width), BF)
    scratch.update(x1s=swap, x1r=swap, x2s=swap, x2r=swap, x3s=swap, x3r=swap, x4s=swap, x4r=swap, lo=swap, ig=swap)
    semaphores = dict(
        local_sem=pltpu.SemaphoreType.DMA((16,)),
        send_sem=pltpu.SemaphoreType.DMA((96,)),
        recv_sem=pltpu.SemaphoreType.DMA((96,)),
    )
    names = [*vectors, *arrays, *outputs, *scratch, *semaphores]
    in_specs = [pl.BlockSpec(memory_space=pltpu.VMEM)] * len(vectors) + [pl.BlockSpec(memory_space=pl.ANY)] * len(arrays)
    return pl.pallas_call(
        functools.partial(layer_kernel, s, names),
        out_shape=[jax.ShapeDtypeStruct(shape, kind) for shape, kind, _ in outputs.values()],
        in_specs=in_specs,
        out_specs=[pl.BlockSpec(memory_space=space) for _, _, space in outputs.values()],
        scratch_shapes=[pltpu.VMEM(shape, kind) for shape, kind in scratch.values()]
        + list(semaphores.values()),
        compiler_params=pltpu.CompilerParams(
            collective_id=0, has_side_effects=True, vmem_limit_bytes=VMEM_LIMIT
        ),
        name="layer",
    )(*vectors.values(), *arrays.values())


def finish_kernel(s, rows, *refs):
    (segments, layer_in, grad_in, grad_mlp, grad_attn, vectors) = refs[:6]
    (
        layer_out,
        input_grad,
        embed,
        fg,
        fs,
        wq,
        qb,
        wk,
        wv,
        vb,
        wo,
        ob,
        sg,
        ss,
        wu,
        ub,
        wd,
        db,
    ) = refs[6:]
    step = pl.program_id(0)
    half = s.rows
    start = longest_start(segments[...], s.docs)
    slots = lax.broadcasted_iota(jnp.int32, (1, half), 1)
    position = lax.broadcasted_iota(jnp.int32, (rows, 1), 0) + step * rows
    choose = [
        jnp.where(packed_source(slots, start, half, block) == position, 1.0, 0.0).astype(BF) for block in range(2)
    ]
    layer_out[...] = (dot(choose[0], layer_in[0]) + dot(choose[1], layer_in[1])).astype(BF)
    grads = dot(choose[0], grad_in[0]) + dot(choose[1], grad_in[1])
    input_grad[...] = grads

    here = segments[0:1, pl.ds(pl.multiple_of(step * rows, rows), rows)]
    docs = jnp.where(lax.broadcasted_iota(jnp.int32, (8, rows), 0) == here, 1.0, 0.0).astype(BF)
    sums = dot(docs, grads.astype(BF))[0 : s.docs]

    @pl.when(step == 0)
    def _():
        embed[0] = sums
        dp_at = lax.axis_index("dp")
        share, width, cols = s.own_share, s.width, s.head_cols
        table = pltpu.roll(vectors[...], lax.rem(width - dp_at * share, width), 1)
        for row, target in enumerate((fg, fs, sg, ss, ob, db, ub)):
            target[...] = table[row : row + 1, 0:share]
        small = cols // s.dp
        heads = pltpu.roll(vectors[...], lax.rem(width - dp_at * small, width), 1)
        qb[...] = heads[7:8, 0:small]
        vb[...] = heads[7:8, 256 : 256 + small]
        wq[...] = grad_attn[0]
        wk[...] = grad_attn[1]
        wv[...] = grad_attn[2]
        wo[...] = grad_attn[3].T
        wu[...] = grad_mlp[0]
        wd[...] = grad_mlp[1]

    @pl.when(step > 0)
    def _():
        embed[0] = embed[0] + sums


def finish_call(s, segments, layer_in, grad_in, grad_mlp, grad_attn, vectors):
    rows = s.length // 4
    width, share, cols, hid = s.width, s.own_share, s.head_cols, s.hidden
    small = cols // s.dp

    def whole(shape):
        return pl.BlockSpec(shape, lambda i: (0,) * len(shape))

    shapes = [
        (s.length, width),
        (s.length, width),
        (1, s.docs, width),
        (1, share),
        (1, share),
        (share, cols),
        (1, small),
        (share, cols),
        (share, cols),
        (1, small),
        (cols, share),
        (1, share),
        (1, share),
        (1, share),
        (share, hid),
        (1, share),
        (share, hid),
        (1, share),
    ]
    by_rows = pl.BlockSpec((rows, width), lambda i: (i, 0))
    return pl.pallas_call(
        functools.partial(finish_kernel, s, rows),
        grid=(s.length // rows,),
        out_shape=[jax.ShapeDtypeStruct(shape, BF if i == 0 else F32) for i, shape in enumerate(shapes)],
        in_specs=[whole(a.shape) for a in (segments, layer_in, grad_in, grad_mlp, grad_attn, vectors)],
        out_specs=[by_rows, by_rows] + [whole(shape) for shape in shapes[2:]],
        compiler_params=pltpu.CompilerParams(vmem_limit_bytes=48 * 2**20),
        name="finish",
    )(segments, layer_in, grad_in, grad_mlp, grad_attn, vectors)


def on_device(
    dp,
    hidden_in,
    document_time_vectors,
    segment_ids,
    first_gain,
    first_shift,
    query_weight,
    query_bias,
    key_weight,
    value_weight,
    value_bias,
    out_weight,
    out_bias,
    second_gain,
    second_shift,
    up_weight,
    up_bias,
    down_weight,
    down_bias,
    cotangent,
):
    length, width = hidden_in.shape
    cols, hidden = query_weight.shape[1], up_weight.shape[1]
    s = Shape(length, width, cols, hidden, document_time_vectors.shape[1], dp, 128)

    vectors = dict(
        segments=segment_ids,
        doc_vectors=document_time_vectors,
        first_gain=first_gain,
        first_shift=first_shift,
        second_gain=second_gain,
        second_shift=second_shift,
        out_bias=out_bias,
        down_bias=down_bias,
        up_bias=up_bias,
        query_bias=query_bias,
        value_bias=value_bias,
    )
    arrays = dict(
        hidden=hidden_in,
        cotangent=cotangent,
        query=query_weight.T,
        key=key_weight.T,
        value=value_weight.T,
        out=out_weight,
        up=up_weight,
        down=down_weight,
    )
    layer_in, grad_in, grad_mlp, grad_attn, vectors = layer_call(s, vectors, arrays)
    if not s.short:
        grad_mlp, grad_attn, vectors = reduce_far(s, grad_mlp, grad_attn, vectors)
    results = finish_call(s, segment_ids, layer_in, grad_in, grad_mlp, grad_attn, vectors)
    results = [y.reshape(y.shape[1]) if y.ndim == 2 and y.shape[0] == 1 else y for y in results]
    results[16] = results[16].T
    return tuple(results)


def reduce_far(s, grad_mlp, grad_attn, vectors):
    mlp = grad_mlp.transpose(2, 0, 1, 3, 4).reshape(2, s.width, s.hidden)
    attn = grad_attn.transpose(2, 0, 1, 3, 4).reshape(4, s.width, s.head_cols)
    return (
        lax.psum_scatter(mlp, "dp", scatter_dimension=1, tiled=True).astype(F32),
        lax.psum_scatter(attn, "dp", scatter_dimension=1, tiled=True).astype(F32),
        lax.psum(vectors, "dp"),
    )


def solution(mesh):
    placed = (
        P("dp", None),
        P("dp", None, None),
        P("dp", None),
        P(),
        P(),
        P(None, "tensor"),
        P("tensor"),
        P(None, "tensor"),
        P(None, "tensor"),
        P("tensor"),
        P("tensor", None),
        P(),
        P(),
        P(),
        P(None, "tensor"),
        P("tensor"),
        P("tensor", None),
        P(),
        P("dp", None),
    )
    return jax.shard_map(
        functools.partial(on_device, mesh.shape["dp"]),
        mesh=mesh,
        in_specs=placed,
        out_specs=(
            P("dp", None),
            P("dp", None),
            P("dp", None, None),
            P("dp"),
            P("dp"),
            P("dp", "tensor"),
            P(("tensor", "dp")),
            P("dp", "tensor"),
            P("dp", "tensor"),
            P(("tensor", "dp")),
            P("tensor", "dp"),
            P("dp"),
            P("dp"),
            P("dp"),
            P("dp", "tensor"),
            P(("tensor", "dp")),
            P("tensor", "dp"),
            P("dp"),
        ),
        check_vma=False,
    )
```

```python
import functools
import math
import types

import jax
import jax.numpy as jnp
from jax import lax
from jax.experimental import pallas as pl
from jax.experimental.pallas import tpu as pltpu
from jax.sharding import PartitionSpec as P

DH = 64
EPSILON = 1e-05
MASKED = -1000000000.0
BF = jnp.bfloat16
F32 = jnp.float32
MESH = pl.DeviceIdType.MESH
VMEM_LIMIT = 67_000_000


def dot(left, right, left_dim=1, right_dim=0):
    return lax.dot_general(
        left, right, (((left_dim,), (right_dim,)), ((), ())), preferred_element_type=F32
    )


def normalize(rows):
    average = jnp.mean(rows, axis=-1, keepdims=True)
    centered = rows - average
    variance = jnp.mean(centered * centered, axis=-1, keepdims=True)
    scale = lax.rsqrt(variance + EPSILON)
    return centered * scale, scale


def norm_back(normal, scale, gain, grad):
    inner = grad * gain
    first = jnp.mean(inner, axis=-1, keepdims=True)
    second = jnp.mean(inner * normal, axis=-1, keepdims=True)
    return scale * (inner - first - normal * second)


def packed_source(slots, start, half, block):
    return (1 - block) * (slots + start) + block * (slots + jnp.where(slots >= start, half, 0))


def longest_start(segments, docs):
    half = segments.shape[1] // 2
    longest = jnp.zeros((1, 1), F32)
    for doc in range(docs):
        count = jnp.sum(jnp.where(segments == doc, 1.0, 0.0), axis=1, keepdims=True)
        longest = longest + jnp.where(count == half, float(doc), 0.0)
    before = jnp.where(segments.astype(F32) < longest, 1.0, 0.0)
    return jnp.sum(before, axis=1, keepdims=True).astype(jnp.int32)


class Shape:
    def __init__(self, length, width, head_cols, hidden, docs, dp):
        self.length, self.width, self.head_cols, self.hidden = length, width, head_cols, hidden
        self.docs, self.dp = docs, dp
        self.rows = length // 2
        self.short = 4 <= dp <= 8 and width // dp % 16 == 0
        blocks = dp if self.short else 8
        self.zs = blocks // 2
        self.share = width // blocks
        self.own_share = width // dp
        self.chunk = self.rows // 4
        self.chunks = 4
        self.heads = head_cols // DH


def layer_kernel(s, names, small_names, *refs):
    r = types.SimpleNamespace(**dict(zip(names, refs)))
    width, n, cols, hidden = s.width, s.rows, s.head_cols, s.hidden
    zs, share, chunk, chunks = s.zs, s.share, s.chunk, s.chunks
    big = 2 * chunk
    dp_at, tensor_at = lax.axis_index("dp"), lax.axis_index("tensor")
    core, side = lax.rem(tensor_at, 2), lax.div(tensor_at, 2)
    x_at, z_at = lax.rem(dp_at, 2), lax.div(dp_at, 2)
    sibling = (dp_at, side * 2 + 1 - core)
    peer = (dp_at, (1 - side) * 2 + core)
    across = (z_at * 2 + 1 - x_at, tensor_at)

    def along(step):
        return (lax.rem(z_at + step, zs) * 2 + x_at, tensor_at)

    def local(source, target, at):
        return pltpu.make_async_copy(source, target, r.local_sem.at[at])

    def remote(source, target, at, device):
        return pltpu.make_async_remote_copy(
            src_ref=source,
            dst_ref=target,
            send_sem=r.send_sem.at[at],
            recv_sem=r.recv_sem.at[at],
            device_id=device,
            device_id_type=MESH,
        )

    WEIGHTS, X1, X2, X3, X4, GRADS, XS, ZS, SUMS, LO, IG = 0, 8, 12, 16, 20, 24, 28, 40, 52, 60, 64
    SMALL, LO_OUT, IG_OUT = 8, 20, 24

    barrier = pltpu.get_barrier_semaphore()
    partners = [sibling, peer]
    if s.short:
        partners = partners + [across] + [along(step) for step in range(1, zs)]
    for partner in partners:
        pl.semaphore_signal(barrier, inc=1, device_id=partner, device_id_type=MESH)

    weights = [
        (r.query, r.wqkv.at[:, 0]),
        (r.key, r.wqkv.at[:, 1]),
        (r.value, r.wqkv.at[:, 2]),
        (r.out, r.wo),
        (r.up, r.wu),
        (r.down, r.wd),
    ]
    small_copies = [
        local(getattr(r, name), getattr(r, "v_" + name), SMALL + i) for i, name in enumerate(small_names)
    ]
    for copy in small_copies:
        copy.start()
    local_hidden = local(r.hidden, r.hid, 0)
    local_hidden.start()
    own_weights = [local(src, dst.at[0], 2 + i) for i, (src, dst) in enumerate(weights)]
    for copy in own_weights[:4]:
        copy.start()
    local_cot = local(r.cotangent, r.cot, 1)
    local_cot.start()
    for copy in own_weights[4:]:
        copy.start()
    for copy in small_copies:
        copy.wait()
    small = r.small
    first_rows = (r.v_first_gain, r.v_first_shift, r.v_second_gain, r.v_second_shift, r.v_out_bias, r.v_down_bias)
    for row, ref in enumerate(first_rows + (None, None, r.v_up_bias, r.v_query_bias, r.v_value_bias)):
        if ref is not None:
            count = ref.shape[0]
            small[row : row + 1, 0:count] = ref[...].reshape(1, count).astype(F32)
    gain_one, shift_one = small[0:1, :], small[1:2, :]
    gain_two, shift_two = small[2:3, :], small[3:4, :]
    out_bias, down_bias = small[4:5, :], small[5:6, :]
    segments = r.v_segments[...]
    start = longest_start(segments, s.docs)
    doc_row = lax.broadcasted_iota(jnp.int32, (8, s.length), 0)
    docs_full = jnp.where(segments == doc_row, 1.0, 0.0).astype(BF)
    doc_vectors = r.v_doc_vectors[0]

    pl.semaphore_wait(barrier, len(partners))
    small_copy = remote(r.small.at[pl.ds(8, 8)], r.small_sib, WEIGHTS + 6, sibling)
    small_copy.start()
    sib_weights = [remote(src, dst.at[1], WEIGHTS + i, sibling) for i, (src, dst) in enumerate(weights)]
    for copy in sib_weights:
        copy.start()

    def at(k, size=chunk):
        return pl.ds(pl.multiple_of(k * size, size), size)

    def choice(k):
        slots = lax.broadcasted_iota(jnp.int32, (big, 1), 0) + k * big
        source = packed_source(slots, start, n, core)
        columns = lax.broadcasted_iota(jnp.int32, (big, s.length), 1)
        return jnp.where(columns == source, 1.0, 0.0).astype(BF)

    local_hidden.wait()
    for copy in own_weights[:3]:
        copy.wait()

    def projections(half, rows, source):
        for j in range(3):
            y = dot(source, r.wqkv[half, j], 1, 1)
            if j != 1:
                bias_row = small if half == 0 else r.small_sib
                base = 8 if half == 0 else 0
                y = y + bias_row[base + 1 + j // 2 : base + 2 + j // 2, 0:cols]
            r.qkv[half, j, rows, :] = y.astype(BF)

    def pack(k, _):
        rows = at(k, big)
        choose = choice(k)
        docs_here = dot(choose, docs_full, 1, 1).astype(BF)
        r.docs[rows, :] = docs_here
        x = dot(choose, r.hid[...]) + dot(docs_here[:, 0 : s.docs], doc_vectors)
        r.resid[rows, :] = x
        normal, _ = normalize(x)
        y = (normal * gain_one + shift_one).astype(BF)
        r.attn_in[rows, :] = y
        projections(0, rows, y)
        return 0

    lax.fori_loop(0, n // big, pack, 0)
    docs_all = r.docs[...]

    small_copy.wait_recv()
    for copy in sib_weights[:3]:
        copy.wait_recv()

    def second_half(k, _):
        rows = at(k, big)
        r.bias[rows, :] = (dot(r.docs[rows, :], docs_all, 1, 1) - 1.0) * (-MASKED)
        projections(1, rows, r.attn_in[rows, :])
        return 0

    lax.fori_loop(0, n // big, second_half, 0)
    own_weights[3].wait()
    sib_weights[3].wait_recv()

    lane = lax.broadcasted_iota(jnp.int32, (1, 128), 1)
    low = jnp.where(lane < DH, 1.0, 0.0)
    high = 1.0 - low
    factor = 1.0 / math.sqrt(DH)
    groups = [(0, 128, (low, high)), (128, 192, (None,))]

    def masked(values, mask, scale=1.0):
        if mask is None:
            return values if scale == 1.0 else values * jnp.asarray(scale, BF)
        return values * (mask * scale).astype(BF)

    def swap(sent, landed, sem, k):
        rows = at(k)
        return remote(sent.at[rows], landed.at[rows], sem + k, peer)

    def forward(k, _):
        rows = at(k)
        bias = r.bias[rows, :]
        for half in range(2):
            for first, last, masks in groups:
                q = r.qkv[half, 0, rows, first:last]
                keys = r.qkv[half, 1, :, first:last]
                values = r.qkv[half, 2, :, first:last]
                mixed = None
                for j, mask in enumerate(masks):
                    head = half * s.heads + first // DH + j
                    scores = dot(masked(q, mask, factor), keys, 1, 1) + bias
                    top = jnp.max(scores, axis=1, keepdims=True)
                    e = jnp.exp(scores - top)
                    total = jnp.sum(e, axis=1, keepdims=True)
                    probs = (e * (1.0 / total)).astype(BF)
                    r.probs[head, rows, :] = probs
                    part = dot(probs, masked(values, mask))
                    mixed = part if mixed is None else mixed + part
                r.mixed32[half, rows, first:last] = mixed
                r.mixed[half, rows, first:last] = mixed.astype(BF)
        partial = dot(r.mixed[0, rows, :], r.wo[0]) + dot(r.mixed[1, rows, :], r.wo[1])
        r.x1s[rows, :] = partial.astype(BF)
        swap(r.x1s, r.x1r, X1, k).start()
        return 0

    lax.fori_loop(0, chunks, forward, 0)

    local_cot.wait()

    def pack_cotangent(k, _):
        r.cotp[at(k, big), :] = dot(choice(k), r.cot[...]).astype(BF)
        return 0

    lax.fori_loop(0, n // big, pack_cotangent, 0)
    r.t2[...] = r.cotp[...].T

    for copy in own_weights[4:]:
        copy.wait()
    for copy in sib_weights[4:]:
        copy.wait_recv()
    up_bias = (small[8:9, :], r.small_sib[0:1, :])
    r.sums[...] = jnp.zeros_like(r.sums[...])

    def add_sum(row, values):
        count = values.shape[1]
        r.sums[row : row + 1, 0:count] = r.sums[row : row + 1, 0:count] + jnp.sum(values, axis=0, keepdims=True)

    def pair(sent, landed, rows):
        return sent[rows, :].astype(F32) + landed[rows, :].astype(F32)

    def mlp(k, _):
        rows = at(k, big)
        for i in range(2):
            swap(r.x1s, r.x1r, X1, 2 * k + i).wait_recv()
        middle = r.resid[rows, :] + pair(r.x1s, r.x1r, rows) + out_bias
        r.middle[rows, :] = middle
        normal, _ = normalize(middle)
        source = (normal * gain_two + shift_two).astype(BF)
        r.mlp_in[rows, :] = source
        grad_top = r.cotp[rows, :]
        add_sum(5, grad_top.astype(F32))
        grad_in = jnp.zeros((big, width), F32)
        for half in range(2):
            r.pre[...] = dot(source, r.wu[half]) + up_bias[half]
            r.dact[...] = dot(grad_top, r.wd[half], 1, 1)

            def gelu(i, _):
                part = pl.ds(pl.multiple_of(i * 16, 16), 16)
                v = r.pre[part, :]
                cdf = 0.5 * (1.0 + lax.erf(v * math.sqrt(0.5)))
                pdf = jnp.exp(-0.5 * v * v) * (1.0 / math.sqrt(2.0 * math.pi))
                where = pl.ds(pl.multiple_of(k * big + i * 16, 16), 16)
                r.act[half, where, :] = (v * cdf).astype(BF)
                r.gpre[half, where, :] = (r.dact[part, :] * (cdf + v * pdf)).astype(BF)
                return 0

            lax.fori_loop(0, big // 16, gelu, 0)
            grad_pre = r.gpre[half, rows, :]
            add_sum(6 + 2 * half, grad_pre.astype(F32))
            grad_in = grad_in + dot(grad_pre, r.wu[half], 1, 1)
        r.x3s[rows, :] = grad_in.astype(BF)
        for i in range(2):
            swap(r.x3s, r.x3r, X3, 2 * k + i).start()
        return 0

    lax.fori_loop(0, n // big, mlp, 0)

    def grad_copy(kind):
        return remote(r.gs.at[kind], r.gr.at[kind], GRADS + kind, sibling)

    def block_grad(kind, left, right, target):
        for part in range(2):
            top = part * (width // 2)
            y = dot(left[top : top + width // 2, :], right)
            target[kind, part * (zs // 2) : (part + 1) * (zs // 2)] = y.astype(BF).reshape(zs // 2, 2, share, hidden)

    r.t1[...] = r.mlp_in[...].T
    for kind, (left, right) in enumerate(((r.t2, r.act), (r.t1, r.gpre))):
        block_grad(kind, left, right[1], r.gs)
        grad_copy(kind).start()
        block_grad(kind, left, right[0], r.go)

    def both(kind, z, which):
        return r.go[kind, z, which].astype(F32) + r.gr[kind, z, which].astype(F32)

    def x_copy(kind, step):
        z = lax.rem(z_at + 1 + step, zs)
        return remote(r.xs.at[kind, z], r.xr.at[kind, z], XS + kind * zs + step, across)

    def z_copy(kind, step):
        return remote(r.zs.at[kind, step], r.zr.at[kind, step], ZS + kind * (zs - 1) + step, along(step + 1))

    def x_stage(kind):
        grad_copy(kind).wait_recv()
        for step in range(zs):
            z = lax.rem(z_at + 1 + step, zs)
            r.xs[kind, z] = both(kind, z, 1 - x_at).astype(BF)
            x_copy(kind, step).start()

    def z_stage(kind):
        for step in range(zs):
            z = lax.rem(z_at + 1 + step, zs)
            x_copy(kind, step).wait_recv()
            y = both(kind, z, x_at) + r.xr[kind, z].astype(F32)
            if step == zs - 1:
                r.grads[kind] = y
            else:
                r.zs[kind, step] = y.astype(BF)
                z_copy(kind, step).start()

    def last_stage(kind):
        y = r.grads[kind]
        for step in range(zs - 1):
            z_copy(kind, step).wait_recv()
            y = y + r.zr[kind, step].astype(F32)
        r.grads[kind] = y

    def whole_sum(kind):
        grad_copy(kind).wait_recv()
        r.grads[kind] = (r.go[kind].astype(F32) + r.gr[kind].astype(F32)).astype(BF)

    for kind in range(2):
        if s.short:
            x_stage(kind)
        else:
            whole_sum(kind)

    def mlp_out(k, _):
        rows = at(k, big)
        part = dot(r.act[0, rows, :], r.wd[0]) + dot(r.act[1, rows, :], r.wd[1])
        r.x2s[rows, :] = part.astype(BF)
        return 0

    lax.fori_loop(0, n // big, mlp_out, 0)
    swap(r.x2s, r.x2r, X2, 0).start()

    r.dk[...] = jnp.zeros_like(r.dk[...])
    r.dv[...] = jnp.zeros_like(r.dv[...])

    def backward(k, _):
        rows = at(k)
        swap(r.x3s, r.x3r, X3, k).wait_recv()
        grad_in = pair(r.x3s, r.x3r, rows)
        normal, scale = normalize(r.middle[rows, :])
        add_sum(2, grad_in * normal)
        add_sum(3, grad_in)
        grad_middle = r.cotp[rows, :].astype(F32) + norm_back(normal, scale, gain_two, grad_in)
        r.gmid[rows, :] = grad_middle
        grad_low = grad_middle.astype(BF)
        r.gml[rows, :] = grad_low
        add_sum(4, grad_low.astype(F32))
        for half in range(2):
            grad_mixed = dot(grad_low, r.wo[half], 1, 1).astype(BF)
            for first, last, masks in groups:
                q = r.qkv[half, 0, rows, first:last]
                keys = r.qkv[half, 1, :, first:last]
                values = r.qkv[half, 2, :, first:last]
                out = grad_mixed[:, first:last]
                product = out.astype(F32) * r.mixed32[half, rows, first:last]
                dq = dk = dv = None
                for j, mask in enumerate(masks):
                    head = half * s.heads + first // DH + j
                    inner = jnp.sum(product if mask is None else product * mask, axis=1, keepdims=True)
                    own_out = masked(out, mask)
                    probs = r.probs[head, rows, :]
                    grad_probs = dot(own_out, values, 1, 1)
                    grad_scores = (probs.astype(F32) * (grad_probs - inner)).astype(BF)
                    parts = (
                        dot(grad_scores, masked(keys, mask, factor)),
                        dot(grad_scores, masked(q, mask, factor), 0, 0),
                        dot(probs, own_out, 0, 0),
                    )
                    if dq is None:
                        dq, dk, dv = parts
                    else:
                        dq, dk, dv = dq + parts[0], dk + parts[1], dv + parts[2]
                r.dqkv[half, 0, rows, first:last] = dq.astype(BF)
                r.dk[half, :, first:last] = r.dk[half, :, first:last] + dk
                r.dv[half, :, first:last] = r.dv[half, :, first:last] + dv
        return 0

    lax.fori_loop(0, chunks, backward, 0)
    r.dqkv[:, 1] = r.dk[...].astype(BF)
    r.dqkv[:, 2] = r.dv[...].astype(BF)

    def attn_in_grad(k, _):
        rows = at(k, big)
        part = jnp.zeros((big, width), F32)
        for half in range(2):
            for j in range(3):
                part = part + dot(r.dqkv[half, j, rows, :], r.wqkv[half, j])
        part = part.astype(BF)
        r.x4s[rows, :] = part
        for i in range(2):
            swap(r.x4s, r.x4r, X4, 2 * k + i).start()
        normal, _ = normalize(r.resid[rows, :])
        add_sum(0, part.astype(F32) * normal)
        add_sum(1, part.astype(F32))
        return 0

    lax.fori_loop(0, n // big, attn_in_grad, 0)
    for k in range(1, chunks):
        swap(r.x2s, r.x2r, X2, k).start()

    for half in range(2):
        add_sum(7 + 2 * half, r.dqkv[half, 0].astype(F32))
        add_sum(10 + half, r.dqkv[half, 2].astype(F32))
    sums_copy = remote(r.sums, r.sums_r, SUMS, sibling)
    sums_copy.start()
    r.t1[...] = r.attn_in[...].T
    r.t2[...] = r.gml[...].T

    def attn_grads(half, target):
        for j in range(4):
            y = dot(r.t1[...], r.dqkv[half, j]) if j < 3 else dot(r.t2[...], r.mixed[half])
            target[2, :, :, :, j * cols : (j + 1) * cols] = y.astype(BF).reshape(zs, 2, share, cols)

    attn_grads(1, r.gs)
    grad_copy(2).start()
    attn_grads(0, r.go)

    sums_copy.wait_recv()
    mine, other = r.sums, r.sums_r
    r.vec[0:6, :] = mine[0:6, :] + other[0:6, :]
    r.vec[6:7, :] = mine[6:7, :] + other[8:9, :]
    r.vec[7:8, :] = jnp.zeros((1, width), F32)
    r.vec[7:8, 0:cols] = mine[7:8, 0:cols] + other[9:10, 0:cols]
    r.vec[7:8, 256 : 256 + cols] = mine[10:11, 0:cols] + other[11:12, 0:cols]
    vec_x = remote(r.vec, r.vec_r, SUMS + 1, across)
    if s.short:
        vec_x.start()
        x_stage(2)
        z_stage(0)
        z_stage(1)
    else:
        whole_sum(2)

    def block_copy(ref, k, sem):
        rows = at(k)
        return remote(ref.at[rows], r.input_grad.at[core, rows], sem + k, sibling)

    def input_grad(k, _):
        rows = at(k)
        swap(r.x4s, r.x4r, X4, k).wait_recv()
        grad_in = pair(r.x4s, r.x4r, rows)
        normal, scale = normalize(r.resid[rows, :])
        y = r.gmid[rows, :] + norm_back(normal, scale, gain_one, grad_in)
        r.ig[rows, :] = y.astype(BF)
        block_copy(r.ig, k, IG).start()
        local(r.ig.at[rows], r.input_grad.at[core, rows], IG_OUT + k).start()
        return 0

    lax.fori_loop(0, chunks, input_grad, 0)

    vec_z = [remote(r.vec2, r.vec_z.at[step], SUMS + 2 + step, along(step + 1)) for step in range(zs - 1)]
    if s.short:
        vec_x.wait_recv()
        r.vec2[...] = r.vec[...] + r.vec_r[...]
        for copy in vec_z:
            copy.start()
        z_stage(2)
        last_stage(0)
        total = r.vec2[...]
        for step, copy in enumerate(vec_z):
            copy.wait_recv()
            total = total + r.vec_z[step]
        r.vec3[...] = total
        last_stage(1)
    else:
        r.vec3[...] = r.vec[...]
    vec_y = remote(r.vec3, r.vec_y, SUMS + 2 + zs, peer)
    vec_y.start()

    def out_copy(k):
        rows = at(k)
        return remote(r.lo.at[core, rows], r.lo.at[core, rows], LO + k, sibling)

    def output(k, _):
        rows = at(k)
        swap(r.x2s, r.x2r, X2, k).wait_recv()
        r.lo[core, rows, :] = (r.middle[rows, :] + pair(r.x2s, r.x2r, rows) + down_bias).astype(BF)
        out_copy(k).start()
        return 0

    lax.fori_loop(0, chunks, output, 0)
    for k in range(chunks):
        out_copy(k).wait_recv()

    def out_local(k):
        rows = at(k, big)
        return local(r.hid.at[rows], r.layer_out.at[rows], LO_OUT + k)

    def unpack(k, _):
        r.hid[at(k, big), :] = unpacked(r.lo, start, n, k, big).astype(BF)
        out_local(k).start()
        return 0

    lax.fori_loop(0, s.length // big, unpack, 0)

    if s.short:
        last_stage(2)
    vec_y.wait_recv()
    r.sums_out[0:2, :] = r.vec3[0:2, :] + r.vec_y[0:2, :]
    r.sums_out[2:8, :] = r.vec3[2:8, :]

    sends = [small_copy, sums_copy, vec_y] + sib_weights + [grad_copy(kind) for kind in range(3)]
    if s.short:
        sends = sends + [vec_x] + vec_z
        for kind in range(3):
            sends = sends + [x_copy(kind, step) for step in range(zs)] + [z_copy(kind, step) for step in range(zs - 1)]
    for copy in sends:
        copy.wait_send()

    def ends(k, _):
        rows = at(k)
        for sent, landed, sem in ((r.x1s, r.x1r, X1), (r.x2s, r.x2r, X2), (r.x3s, r.x3r, X3), (r.x4s, r.x4r, X4)):
            swap(sent, landed, sem, k).wait_send()
        out_copy(k).wait_send()
        out_local(k).wait()
        block_copy(r.ig, k, IG).wait()
        local(r.ig.at[rows], r.input_grad.at[core, rows], IG_OUT + k).wait()
        return 0

    lax.fori_loop(0, chunks, ends, 0)


def unpacked(packed, start, n, k, size):
    position = lax.broadcasted_iota(jnp.int32, (size, 1), 0) + k * size
    slots = lax.broadcasted_iota(jnp.int32, (size, n), 1)
    choose = jnp.where(slots + start == position, 1.0, 0.0).astype(BF)
    inside = jnp.where(position >= start, 1.0, 0.0) * jnp.where(position < start + n, 1.0, 0.0)
    rest = packed[1, pl.ds(pl.multiple_of(lax.rem(k * size, n), size), size), :].astype(F32)
    return jnp.where(inside > 0.5, dot(choose, packed[0]), rest)


def layer_call(s, vectors, arrays):
    n, width, cols, hid = s.rows, s.width, s.head_cols, s.hidden
    zs, share, big = s.zs, s.share, 2 * s.chunk
    outputs = dict(
        layer_out=((s.length, width), BF, pl.ANY),
        input_grad=((2, n, width), BF, pl.ANY),
        grads=((3, share, hid) if s.short else (3, zs, 2, share, hid), F32 if s.short else BF, pltpu.VMEM),
        sums_out=((8, width), F32, pltpu.VMEM),
    )
    swapped = ((n, width), BF)
    rows32 = ((n, width), F32)
    blocks = ((3, zs, 2, share, hid), BF)
    table = ((8, width), F32)
    scratch = dict(
        hid=((s.length, width), BF),
        cot=((s.length, width), BF),
        wqkv=((2, 3, cols, width), BF),
        wo=((2, cols, width), BF),
        wu=((2, width, hid), BF),
        wd=((2, hid, width), BF),
        small=((16, width), F32),
        small_sib=table,
        docs=((n, 8), BF),
        bias=((n, n), F32),
        resid=rows32,
        attn_in=swapped,
        cotp=swapped,
        qkv=((2, 3, n, cols), BF),
        probs=((2 * s.heads, n, n), BF),
        mixed32=((2, n, cols), F32),
        mixed=((2, n, cols), BF),
        middle=rows32,
        mlp_in=swapped,
        act=((2, n, hid), BF),
        gpre=((2, n, hid), BF),
        pre=((big, hid), F32),
        dact=((big, hid), F32),
        gmid=rows32,
        gml=swapped,
        dk=((2, n, cols), F32),
        dv=((2, n, cols), F32),
        dqkv=((2, 3, n, cols), BF),
        t1=((width, n), BF),
        t2=((width, n), BF),
        gs=blocks,
        go=blocks,
        gr=blocks,
        sums=((16, width), F32),
        sums_r=((16, width), F32),
        vec=table,
        vec3=table,
        vec_y=table,
        x1s=swapped,
        x1r=swapped,
        x2s=swapped,
        x2r=swapped,
        x3s=swapped,
        x3r=swapped,
        x4s=swapped,
        x4r=swapped,
        lo=((2, n, width), BF),
        ig=swapped,
    )
    if s.short:
        scratch.update(
            xs=((3, zs, share, hid), BF),
            xr=((3, zs, share, hid), BF),
            zs=((3, zs - 1, share, hid), BF),
            zr=((3, zs - 1, share, hid), BF),
        )
    scratch.update(vec_r=table, vec2=table, vec_z=((zs - 1, 8, width), F32))
    for name, value in vectors.items():
        scratch["v_" + name] = (value.shape, value.dtype)
    semaphores = dict(
        local_sem=pltpu.SemaphoreType.DMA((32,)),
        send_sem=pltpu.SemaphoreType.DMA((72,)),
        recv_sem=pltpu.SemaphoreType.DMA((72,)),
    )
    names = [*vectors, *arrays, *outputs, *scratch, *semaphores]
    return pl.pallas_call(
        functools.partial(layer_kernel, s, names, list(vectors)),
        out_shape=[jax.ShapeDtypeStruct(shape, kind) for shape, kind, _ in outputs.values()],
        in_specs=[pl.BlockSpec(memory_space=pl.ANY)] * (len(vectors) + len(arrays)),
        out_specs=[pl.BlockSpec(memory_space=space) for _, _, space in outputs.values()],
        scratch_shapes=[pltpu.VMEM(shape, kind) for shape, kind in scratch.values()] + list(semaphores.values()),
        compiler_params=pltpu.CompilerParams(
            collective_id=0, has_side_effects=True, vmem_limit_bytes=VMEM_LIMIT
        ),
        name="layer",
    )(*vectors.values(), *arrays.values())


def finish_kernel(s, names, *refs):
    r = types.SimpleNamespace(**dict(zip(names, refs)))
    n, width, cols, share = s.rows, s.width, s.head_cols, s.own_share
    size = n // 2

    def copy(source, target, at):
        return pltpu.make_async_copy(source, target, r.sem.at[at])

    seg_in = copy(r.segments, r.seg, 15)
    seg_in.start()
    ig_in = copy(r.grad_in, r.packed, 0)
    ig_in.start()
    lo_in = copy(r.layer_in, r.lo, 1)
    lo_in.start()
    grads_in = [copy(r.grads.at[kind], r.held.at[kind], 2 + kind) for kind in range(3)]
    for one in grads_in:
        one.start()
    sums_in = copy(r.sums, r.table, 14)
    sums_in.start()
    seg_in.wait()
    start = longest_start(r.seg[...], s.docs)
    r.embed[...] = jnp.zeros_like(r.embed[...])
    lo_out = copy(r.lo, r.layer_out, 1)
    wd_out = copy(r.held.at[0], r.wd, 2)
    wu_out = copy(r.held.at[1], r.wu, 3)
    ig_in.wait()

    def ig_out(k):
        rows = pl.ds(pl.multiple_of(k * size, size), size)
        return copy(r.rows_out.at[rows], r.input_grad.at[rows], 8 + k)

    def unpack(k, _):
        rows = pl.ds(pl.multiple_of(k * size, size), size)
        y = unpacked(r.packed, start, n, k, size)
        r.rows_out[rows, :] = y
        ig_out(k).start()
        docs = jnp.where(lax.broadcasted_iota(jnp.int32, (8, size), 0) == r.seg[0:1, rows], 1.0, 0.0).astype(BF)
        r.embed[0] = r.embed[0] + dot(docs, y.astype(BF))[0 : s.docs]
        return 0

    unpack(0, 0)
    lo_in.wait()
    lo_out.start()
    lax.fori_loop(1, s.length // size, unpack, 0)
    grads_in[0].wait()
    wd_out.start()
    grads_in[1].wait()
    wu_out.start()
    dp_at = lax.axis_index("dp")
    sums_in.wait()
    table = pltpu.roll(r.table[...], lax.rem(width - dp_at * share, width), 1)
    for row, target in enumerate((r.fg, r.fs, r.sg, r.ss, r.ob, r.db, r.ub)):
        target[...] = table[row : row + 1, 0:share]
    small = cols // s.dp
    heads = pltpu.roll(r.table[...], lax.rem(width - dp_at * small, width), 1)
    r.qb[...] = heads[7:8, 0:small]
    r.vb[...] = heads[7:8, 256 : 256 + small]
    grads_in[2].wait()
    attn = r.held[2]
    r.wq[...] = attn[:, 0:cols]
    r.wk[...] = attn[:, cols : 2 * cols]
    r.wv[...] = attn[:, 2 * cols : 3 * cols]
    r.wo[...] = attn[:, 3 * cols : 4 * cols].T
    lo_out.wait()
    wd_out.wait()
    wu_out.wait()
    for k in range(s.length // size):
        ig_out(k).wait()


def finish_call(s, segments, layer_in, grad_in, grads, sums):
    width, share, cols, hid = s.width, s.own_share, s.head_cols, s.hidden
    small = cols // s.dp
    arrays = dict(segments=segments, layer_in=layer_in, grad_in=grad_in, grads=grads, sums=sums)
    outputs = dict(
        layer_out=(s.length, width),
        input_grad=(s.length, width),
        embed=(1, s.docs, width),
        fg=(1, share),
        fs=(1, share),
        wq=(share, cols),
        qb=(1, small),
        wk=(share, cols),
        wv=(share, cols),
        vb=(1, small),
        wo=(cols, share),
        ob=(1, share),
        sg=(1, share),
        ss=(1, share),
        wu=(share, hid),
        ub=(1, share),
        wd=(share, hid),
        db=(1, share),
    )
    far = ("layer_out", "input_grad", "wu", "wd")
    scratch = dict(
        seg=(segments.shape, segments.dtype),
        packed=(grad_in.shape, BF),
        lo=(layer_in.shape, BF),
        rows_out=((s.length, width), F32),
        held=(grads.shape, F32),
        table=(sums.shape, F32),
    )
    names = [*arrays, *outputs, *scratch, "sem"]
    return pl.pallas_call(
        functools.partial(finish_kernel, s, names),
        out_shape=[
            jax.ShapeDtypeStruct(shape, BF if name == "layer_out" else F32) for name, shape in outputs.items()
        ],
        in_specs=[pl.BlockSpec(memory_space=pl.ANY)] * len(arrays),
        out_specs=[pl.BlockSpec(memory_space=pl.ANY if name in far else pltpu.VMEM) for name in outputs],
        scratch_shapes=[pltpu.VMEM(shape, kind) for shape, kind in scratch.values()]
        + [pltpu.SemaphoreType.DMA((16,))],
        compiler_params=pltpu.CompilerParams(vmem_limit_bytes=VMEM_LIMIT),
        name="finish",
    )(*arrays.values())


def on_device(
    dp,
    hidden_in,
    document_time_vectors,
    segment_ids,
    first_gain,
    first_shift,
    query_weight,
    query_bias,
    key_weight,
    value_weight,
    value_bias,
    out_weight,
    out_bias,
    second_gain,
    second_shift,
    up_weight,
    up_bias,
    down_weight,
    down_bias,
    cotangent,
):
    length, width = hidden_in.shape
    cols, hidden = query_weight.shape[1], up_weight.shape[1]
    s = Shape(length, width, cols, hidden, document_time_vectors.shape[1], dp)

    vectors = dict(
        segments=segment_ids,
        doc_vectors=document_time_vectors,
        first_gain=first_gain,
        first_shift=first_shift,
        second_gain=second_gain,
        second_shift=second_shift,
        out_bias=out_bias,
        down_bias=down_bias,
        up_bias=up_bias,
        query_bias=query_bias,
        value_bias=value_bias,
    )
    arrays = dict(
        hidden=hidden_in,
        cotangent=cotangent,
        query=query_weight.T,
        key=key_weight.T,
        value=value_weight.T,
        out=out_weight,
        up=up_weight,
        down=down_weight,
    )
    layer_out, input_grad, grads, sums = layer_call(s, vectors, arrays)
    if not s.short:
        grads = grads.reshape(3, width, width)
        grads = lax.psum_scatter(grads, "dp", scatter_dimension=1, tiled=True).astype(F32)
        sums = lax.psum(sums, "dp")
    results = finish_call(s, segment_ids, layer_out, input_grad, grads, sums)
    results = [y.reshape(y.shape[1]) if y.ndim == 2 and y.shape[0] == 1 else y for y in results]
    results[16] = results[16].T
    return tuple(results)


def solution(mesh):
    placed = (
        P("dp", None),
        P("dp", None, None),
        P("dp", None),
        P(),
        P(),
        P(None, "tensor"),
        P("tensor"),
        P(None, "tensor"),
        P(None, "tensor"),
        P("tensor"),
        P("tensor", None),
        P(),
        P(),
        P(),
        P(None, "tensor"),
        P("tensor"),
        P("tensor", None),
        P(),
        P("dp", None),
    )
    return jax.shard_map(
        functools.partial(on_device, mesh.shape["dp"]),
        mesh=mesh,
        in_specs=placed,
        out_specs=(
            P("dp", None),
            P("dp", None),
            P("dp", None, None),
            P("dp"),
            P("dp"),
            P("dp", "tensor"),
            P(("tensor", "dp")),
            P("dp", "tensor"),
            P("dp", "tensor"),
            P(("tensor", "dp")),
            P("tensor", "dp"),
            P("dp"),
            P("dp"),
            P("dp"),
            P("dp", "tensor"),
            P(("tensor", "dp")),
            P("tensor", "dp"),
            P("dp"),
        ),
        check_vma=False,
    )
```

```python
import functools
import math
import types

import jax
import jax.numpy as jnp
from jax import lax
from jax.experimental import pallas as pl
from jax.experimental.pallas import tpu as pltpu
from jax.sharding import PartitionSpec as P

DH = 64
EPSILON = 1e-05
MASKED = -1000000000.0
BF = jnp.bfloat16
F32 = jnp.float32
MESH = pl.DeviceIdType.MESH
VMEM_LIMIT = 67_000_000


def dot(left, right, left_dim=1, right_dim=0):
    return lax.dot_general(
        left, right, (((left_dim,), (right_dim,)), ((), ())), preferred_element_type=F32
    )


def normalize(rows):
    average = jnp.mean(rows, axis=-1, keepdims=True)
    centered = rows - average
    variance = jnp.mean(centered * centered, axis=-1, keepdims=True)
    scale = lax.rsqrt(variance + EPSILON)
    return centered * scale, scale


def norm_back(normal, scale, gain, grad):
    inner = grad * gain
    first = jnp.mean(inner, axis=-1, keepdims=True)
    second = jnp.mean(inner * normal, axis=-1, keepdims=True)
    return scale * (inner - first - normal * second)


def packed_source(slots, start, half, block):
    return (1 - block) * (slots + start) + block * (slots + jnp.where(slots >= start, half, 0))


def longest_start(segments, docs):
    half = segments.shape[1] // 2
    longest = jnp.zeros((1, 1), F32)
    for doc in range(docs):
        count = jnp.sum(jnp.where(segments == doc, 1.0, 0.0), axis=1, keepdims=True)
        longest = longest + jnp.where(count == half, float(doc), 0.0)
    before = jnp.where(segments.astype(F32) < longest, 1.0, 0.0)
    return jnp.sum(before, axis=1, keepdims=True).astype(jnp.int32)


class Shape:
    def __init__(self, length, width, head_cols, hidden, docs, dp):
        self.length, self.width, self.head_cols, self.hidden = length, width, head_cols, hidden
        self.docs, self.dp = docs, dp
        self.rows = length // 2
        self.short = 4 <= dp <= 8 and width // dp % 16 == 0
        blocks = dp if self.short else 8
        self.zs = blocks // 2
        self.share = width // blocks
        self.own_share = width // dp
        self.chunk = self.rows // 4
        self.chunks = 4
        self.heads = head_cols // DH


def layer_kernel(s, names, small_names, *refs):
    r = types.SimpleNamespace(**dict(zip(names, refs)))
    width, n, cols, hidden = s.width, s.rows, s.head_cols, s.hidden
    zs, share, chunk, chunks = s.zs, s.share, s.chunk, s.chunks
    big = 2 * chunk
    dp_at, tensor_at = lax.axis_index("dp"), lax.axis_index("tensor")
    core, side = lax.rem(tensor_at, 2), lax.div(tensor_at, 2)
    x_at, z_at = lax.rem(dp_at, 2), lax.div(dp_at, 2)
    sibling = (dp_at, side * 2 + 1 - core)
    peer = (dp_at, (1 - side) * 2 + core)
    across = (z_at * 2 + 1 - x_at, tensor_at)

    def along(step):
        return (lax.rem(z_at + step, zs) * 2 + x_at, tensor_at)

    def local(source, target, at):
        return pltpu.make_async_copy(source, target, r.local_sem.at[at])

    def remote(source, target, at, device):
        return pltpu.make_async_remote_copy(
            src_ref=source,
            dst_ref=target,
            send_sem=r.send_sem.at[at],
            recv_sem=r.recv_sem.at[at],
            device_id=device,
            device_id_type=MESH,
        )

    WEIGHTS, X1, X2, X3, X4, GRADS, XS, ZS, SUMS, LO, IG = 0, 8, 12, 16, 20, 24, 28, 40, 52, 60, 64
    SMALL, LO_OUT, IG_OUT = 8, 20, 24

    barrier = pltpu.get_barrier_semaphore()
    partners = [sibling, peer]
    if s.short:
        partners = partners + [across] + [along(step) for step in range(1, zs)]
    for partner in partners:
        pl.semaphore_signal(barrier, inc=1, device_id=partner, device_id_type=MESH)

    weights = [
        (r.query, r.wqkv.at[:, 0]),
        (r.key, r.wqkv.at[:, 1]),
        (r.value, r.wqkv.at[:, 2]),
        (r.out, r.wo),
        (r.up, r.wu),
        (r.down, r.wd),
    ]
    small_copies = [
        local(getattr(r, name), getattr(r, "v_" + name), SMALL + i) for i, name in enumerate(small_names)
    ]
    for copy in small_copies:
        copy.start()
    local_hidden = local(r.hidden, r.hid, 0)
    local_hidden.start()
    own_weights = [local(src, dst.at[0], 2 + i) for i, (src, dst) in enumerate(weights)]
    for copy in own_weights[:4]:
        copy.start()
    local_cot = local(r.cotangent, r.cot, 1)
    local_cot.start()
    for copy in own_weights[4:]:
        copy.start()
    for copy in small_copies:
        copy.wait()
    small = r.small
    first_rows = (r.v_first_gain, r.v_first_shift, r.v_second_gain, r.v_second_shift, r.v_out_bias, r.v_down_bias)
    for row, ref in enumerate(first_rows + (None, None, r.v_up_bias, r.v_query_bias, r.v_value_bias)):
        if ref is not None:
            count = ref.shape[0]
            small[row : row + 1, 0:count] = ref[...].reshape(1, count).astype(F32)
    gain_one, shift_one = small[0:1, :], small[1:2, :]
    gain_two, shift_two = small[2:3, :], small[3:4, :]
    out_bias, down_bias = small[4:5, :], small[5:6, :]
    segments = r.v_segments[...]
    start = longest_start(segments, s.docs)
    doc_row = lax.broadcasted_iota(jnp.int32, (8, s.length), 0)
    docs_full = jnp.where(segments == doc_row, 1.0, 0.0).astype(BF)
    doc_vectors = r.v_doc_vectors[0]

    pl.semaphore_wait(barrier, len(partners))
    small_copy = remote(r.small.at[pl.ds(8, 8)], r.small_sib, WEIGHTS + 6, sibling)
    small_copy.start()
    sib_weights = [remote(src, dst.at[1], WEIGHTS + i, sibling) for i, (src, dst) in enumerate(weights)]
    for copy in sib_weights:
        copy.start()

    def at(k, size=chunk):
        return pl.ds(pl.multiple_of(k * size, size), size)

    def choice(k):
        slots = lax.broadcasted_iota(jnp.int32, (big, 1), 0) + k * big
        source = packed_source(slots, start, n, core)
        columns = lax.broadcasted_iota(jnp.int32, (big, s.length), 1)
        return jnp.where(columns == source, 1.0, 0.0).astype(BF)

    local_hidden.wait()
    for copy in own_weights[:3]:
        copy.wait()

    def projections(half, rows, source):
        for j in range(3):
            y = dot(source, r.wqkv[half, j], 1, 1)
            if j != 1:
                bias_row = small if half == 0 else r.small_sib
                base = 8 if half == 0 else 0
                y = y + bias_row[base + 1 + j // 2 : base + 2 + j // 2, 0:cols]
            r.qkv[half, j, rows, :] = y.astype(BF)

    def pack(k, _):
        rows = at(k, big)
        choose = choice(k)
        docs_here = dot(choose, docs_full, 1, 1).astype(BF)
        r.docs[rows, :] = docs_here
        x = dot(choose, r.hid[...]) + dot(docs_here[:, 0 : s.docs], doc_vectors)
        r.resid[rows, :] = x
        normal, _ = normalize(x)
        y = (normal * gain_one + shift_one).astype(BF)
        r.attn_in[rows, :] = y
        projections(0, rows, y)
        return 0

    lax.fori_loop(0, n // big, pack, 0)
    docs_all = r.docs[...]

    small_copy.wait_recv()
    for copy in sib_weights[:3]:
        copy.wait_recv()

    def second_half(k, _):
        rows = at(k, big)
        r.bias[rows, :] = (dot(r.docs[rows, :], docs_all, 1, 1) - 1.0) * (-MASKED)
        projections(1, rows, r.attn_in[rows, :])
        return 0

    lax.fori_loop(0, n // big, second_half, 0)
    own_weights[3].wait()
    sib_weights[3].wait_recv()

    lane = lax.broadcasted_iota(jnp.int32, (1, 128), 1)
    low = jnp.where(lane < DH, 1.0, 0.0)
    high = 1.0 - low
    factor = 1.0 / math.sqrt(DH)
    groups = [(0, 128, (low, high)), (128, 192, (None,))]

    def masked(values, mask, scale=1.0):
        if mask is None:
            return values if scale == 1.0 else values * jnp.asarray(scale, BF)
        return values * (mask * scale).astype(BF)

    def swap(sent, landed, sem, k):
        rows = at(k)
        return remote(sent.at[rows], landed.at[rows], sem + k, peer)

    def forward(k, _):
        rows = at(k)
        bias = r.bias[rows, :]
        for half in range(2):
            for first, last, masks in groups:
                q = r.qkv[half, 0, rows, first:last]
                keys = r.qkv[half, 1, :, first:last]
                values = r.qkv[half, 2, :, first:last]
                mixed = None
                for j, mask in enumerate(masks):
                    head = half * s.heads + first // DH + j
                    scores = dot(masked(q, mask, factor), keys, 1, 1) + bias
                    top = jnp.max(scores, axis=1, keepdims=True)
                    e = jnp.exp(scores - top)
                    total = jnp.sum(e, axis=1, keepdims=True)
                    probs = (e * (1.0 / total)).astype(BF)
                    r.probs[head, rows, :] = probs
                    part = dot(probs, masked(values, mask))
                    mixed = part if mixed is None else mixed + part
                r.mixed32[half, rows, first:last] = mixed
                r.mixed[half, rows, first:last] = mixed.astype(BF)
        partial = dot(r.mixed[0, rows, :], r.wo[0]) + dot(r.mixed[1, rows, :], r.wo[1])
        r.x1s[rows, :] = partial.astype(BF)
        swap(r.x1s, r.x1r, X1, k).start()
        return 0

    lax.fori_loop(0, chunks, forward, 0)

    local_cot.wait()

    def pack_cotangent(k, _):
        r.cotp[at(k, big), :] = dot(choice(k), r.cot[...]).astype(BF)
        return 0

    lax.fori_loop(0, n // big, pack_cotangent, 0)
    r.t2[...] = r.cotp[...].T

    for copy in own_weights[4:]:
        copy.wait()
    for copy in sib_weights[4:]:
        copy.wait_recv()
    up_bias = (small[8:9, :], r.small_sib[0:1, :])
    r.sums[...] = jnp.zeros_like(r.sums[...])

    def add_sum(row, values):
        count = values.shape[1]
        r.sums[row : row + 1, 0:count] = r.sums[row : row + 1, 0:count] + jnp.sum(values, axis=0, keepdims=True)

    def pair(sent, landed, rows):
        return sent[rows, :].astype(F32) + landed[rows, :].astype(F32)

    def mlp(k, _):
        rows = at(k, big)
        for i in range(2):
            swap(r.x1s, r.x1r, X1, 2 * k + i).wait_recv()
        middle = r.resid[rows, :] + pair(r.x1s, r.x1r, rows) + out_bias
        r.middle[rows, :] = middle
        normal, _ = normalize(middle)
        source = (normal * gain_two + shift_two).astype(BF)
        r.mlp_in[rows, :] = source
        grad_top = r.cotp[rows, :]
        add_sum(5, grad_top.astype(F32))
        grad_in = jnp.zeros((big, width), F32)
        for half in range(2):
            r.pre[...] = dot(source, r.wu[half]) + up_bias[half]
            r.dact[...] = dot(grad_top, r.wd[half], 1, 1)

            def gelu(i, _):
                part = pl.ds(pl.multiple_of(i * 16, 16), 16)
                v = r.pre[part, :]
                cdf = 0.5 * (1.0 + lax.erf(v * math.sqrt(0.5)))
                pdf = jnp.exp(-0.5 * v * v) * (1.0 / math.sqrt(2.0 * math.pi))
                where = pl.ds(pl.multiple_of(k * big + i * 16, 16), 16)
                r.act[half, where, :] = (v * cdf).astype(BF)
                r.gpre[half, where, :] = (r.dact[part, :] * (cdf + v * pdf)).astype(BF)
                return 0

            lax.fori_loop(0, big // 16, gelu, 0)
            grad_pre = r.gpre[half, rows, :]
            add_sum(6 + 2 * half, grad_pre.astype(F32))
            grad_in = grad_in + dot(grad_pre, r.wu[half], 1, 1)
        r.x3s[rows, :] = grad_in.astype(BF)
        for i in range(2):
            swap(r.x3s, r.x3r, X3, 2 * k + i).start()
        return 0

    lax.fori_loop(0, n // big, mlp, 0)

    def grad_copy(kind):
        return remote(r.gs.at[kind], r.gr.at[kind], GRADS + kind, sibling)

    def block_grad(kind, left, right, target):
        for part in range(2):
            top = part * (width // 2)
            y = dot(left[top : top + width // 2, :], right)
            target[kind, part * (zs // 2) : (part + 1) * (zs // 2)] = y.astype(BF).reshape(zs // 2, 2, share, hidden)

    r.t1[...] = r.mlp_in[...].T
    for kind, (left, right) in enumerate(((r.t2, r.act), (r.t1, r.gpre))):
        block_grad(kind, left, right[1], r.gs)
        grad_copy(kind).start()
        block_grad(kind, left, right[0], r.go)

    def both(kind, z, which):
        return r.go[kind, z, which].astype(F32) + r.gr[kind, z, which].astype(F32)

    def x_copy(kind, step):
        z = lax.rem(z_at + 1 + step, zs)
        return remote(r.xs.at[kind, z], r.xr.at[kind, z], XS + kind * zs + step, across)

    def z_copy(kind, step):
        return remote(r.zs.at[kind, step], r.zr.at[kind, step], ZS + kind * (zs - 1) + step, along(step + 1))

    def x_stage(kind):
        grad_copy(kind).wait_recv()
        for step in range(zs):
            z = lax.rem(z_at + 1 + step, zs)
            r.xs[kind, z] = both(kind, z, 1 - x_at).astype(BF)
            x_copy(kind, step).start()

    def x_sum(kind, step):
        z = lax.rem(z_at + 1 + step, zs)
        x_copy(kind, step).wait_recv()
        return both(kind, z, x_at) + r.xr[kind, z].astype(F32)

    def z_step(kind, step):
        r.zs[kind, step] = x_sum(kind, step).astype(BF)
        z_copy(kind, step).start()

    def z_stage(kind, first=0):
        for step in range(first, zs - 1):
            z_step(kind, step)
        r.grads[kind] = x_sum(kind, zs - 1)

    def last_stage(kind):
        y = r.grads[kind]
        for step in range(zs - 1):
            z_copy(kind, step).wait_recv()
            y = y + r.zr[kind, step].astype(F32)
        r.grads[kind] = y

    def whole_sum(kind):
        grad_copy(kind).wait_recv()
        r.grads[kind] = (r.go[kind].astype(F32) + r.gr[kind].astype(F32)).astype(BF)

    for kind in range(2):
        if s.short:
            x_stage(kind)
        else:
            whole_sum(kind)

    def mlp_out(k, _):
        rows = at(k, big)
        part = dot(r.act[0, rows, :], r.wd[0]) + dot(r.act[1, rows, :], r.wd[1])
        r.x2s[rows, :] = part.astype(BF)
        return 0

    lax.fori_loop(0, n // big, mlp_out, 0)
    swap(r.x2s, r.x2r, X2, 0).start()

    r.dk[...] = jnp.zeros_like(r.dk[...])
    r.dv[...] = jnp.zeros_like(r.dv[...])

    def backward(k, _):
        rows = at(k)
        swap(r.x3s, r.x3r, X3, k).wait_recv()
        grad_in = pair(r.x3s, r.x3r, rows)
        normal, scale = normalize(r.middle[rows, :])
        add_sum(2, grad_in * normal)
        add_sum(3, grad_in)
        grad_middle = r.cotp[rows, :].astype(F32) + norm_back(normal, scale, gain_two, grad_in)
        r.gmid[rows, :] = grad_middle
        grad_low = grad_middle.astype(BF)
        r.gml[rows, :] = grad_low
        add_sum(4, grad_low.astype(F32))
        for half in range(2):
            grad_mixed = dot(grad_low, r.wo[half], 1, 1).astype(BF)
            for first, last, masks in groups:
                q = r.qkv[half, 0, rows, first:last]
                keys = r.qkv[half, 1, :, first:last]
                values = r.qkv[half, 2, :, first:last]
                out = grad_mixed[:, first:last]
                product = out.astype(F32) * r.mixed32[half, rows, first:last]
                dq = dk = dv = None
                for j, mask in enumerate(masks):
                    head = half * s.heads + first // DH + j
                    inner = jnp.sum(product if mask is None else product * mask, axis=1, keepdims=True)
                    own_out = masked(out, mask)
                    probs = r.probs[head, rows, :]
                    grad_probs = dot(own_out, values, 1, 1)
                    grad_scores = (probs.astype(F32) * (grad_probs - inner)).astype(BF)
                    parts = (
                        dot(grad_scores, masked(keys, mask, factor)),
                        dot(grad_scores, masked(q, mask, factor), 0, 0),
                        dot(probs, own_out, 0, 0),
                    )
                    if dq is None:
                        dq, dk, dv = parts
                    else:
                        dq, dk, dv = dq + parts[0], dk + parts[1], dv + parts[2]
                r.dqkv[half, 0, rows, first:last] = dq.astype(BF)
                r.dk[half, :, first:last] = r.dk[half, :, first:last] + dk
                r.dv[half, :, first:last] = r.dv[half, :, first:last] + dv
        if s.short:

            @pl.when(k < zs - 1)
            def _():
                z_step(0, k)

        return 0

    lax.fori_loop(0, chunks, backward, 0)
    r.dqkv[:, 1] = r.dk[...].astype(BF)
    r.dqkv[:, 2] = r.dv[...].astype(BF)

    def attn_in_grad(k, _):
        rows = at(k, big)
        part = jnp.zeros((big, width), F32)
        for half in range(2):
            for j in range(3):
                part = part + dot(r.dqkv[half, j, rows, :], r.wqkv[half, j])
        part = part.astype(BF)
        r.x4s[rows, :] = part
        for i in range(2):
            swap(r.x4s, r.x4r, X4, 2 * k + i).start()
        normal, _ = normalize(r.resid[rows, :])
        add_sum(0, part.astype(F32) * normal)
        add_sum(1, part.astype(F32))
        return 0

    lax.fori_loop(0, n // big, attn_in_grad, 0)
    for k in range(1, chunks):
        swap(r.x2s, r.x2r, X2, k).start()

    for half in range(2):
        add_sum(7 + 2 * half, r.dqkv[half, 0].astype(F32))
        add_sum(10 + half, r.dqkv[half, 2].astype(F32))
    sums_copy = remote(r.sums, r.sums_r, SUMS, sibling)
    sums_copy.start()
    r.t1[...] = r.attn_in[...].T
    r.t2[...] = r.gml[...].T

    def attn_grads(half, target):
        for j in range(4):
            y = dot(r.t1[...], r.dqkv[half, j]) if j < 3 else dot(r.t2[...], r.mixed[half])
            target[2, :, :, :, j * cols : (j + 1) * cols] = y.astype(BF).reshape(zs, 2, share, cols)

    attn_grads(1, r.gs)
    grad_copy(2).start()
    if s.short:
        z_stage(0, zs - 1)
        z_step(1, 0)
    attn_grads(0, r.go)

    sums_copy.wait_recv()
    mine, other = r.sums, r.sums_r
    r.vec[0:6, :] = mine[0:6, :] + other[0:6, :]
    r.vec[6:7, :] = mine[6:7, :] + other[8:9, :]
    r.vec[7:8, :] = jnp.zeros((1, width), F32)
    r.vec[7:8, 0:cols] = mine[7:8, 0:cols] + other[9:10, 0:cols]
    r.vec[7:8, 256 : 256 + cols] = mine[10:11, 0:cols] + other[11:12, 0:cols]
    vec_x = remote(r.vec, r.vec_r, SUMS + 1, across)
    if s.short:
        vec_x.start()
        x_stage(2)
        z_stage(1, 1)
    else:
        whole_sum(2)

    def block_copy(ref, k, sem):
        rows = at(k)
        return remote(ref.at[rows], r.input_grad.at[core, rows], sem + k, sibling)

    def input_grad(k, _):
        rows = at(k)
        swap(r.x4s, r.x4r, X4, k).wait_recv()
        grad_in = pair(r.x4s, r.x4r, rows)
        normal, scale = normalize(r.resid[rows, :])
        y = r.gmid[rows, :] + norm_back(normal, scale, gain_one, grad_in)
        r.ig[rows, :] = y.astype(BF)
        block_copy(r.ig, k, IG).start()
        local(r.ig.at[rows], r.input_grad.at[core, rows], IG_OUT + k).start()
        return 0

    lax.fori_loop(0, chunks, input_grad, 0)

    vec_z = [remote(r.vec2, r.vec_z.at[step], SUMS + 2 + step, along(step + 1)) for step in range(zs - 1)]
    if s.short:
        vec_x.wait_recv()
        r.vec2[...] = r.vec[...] + r.vec_r[...]
        for copy in vec_z:
            copy.start()
        z_stage(2)
        last_stage(0)
        total = r.vec2[...]
        for step, copy in enumerate(vec_z):
            copy.wait_recv()
            total = total + r.vec_z[step]
        r.vec3[...] = total
        last_stage(1)
    else:
        r.vec3[...] = r.vec[...]
    vec_y = remote(r.vec3, r.vec_y, SUMS + 2 + zs, peer)
    vec_y.start()

    def out_copy(k):
        rows = at(k)
        return remote(r.lo.at[core, rows], r.lo.at[core, rows], LO + k, sibling)

    def output(k, _):
        rows = at(k)
        swap(r.x2s, r.x2r, X2, k).wait_recv()
        r.lo[core, rows, :] = (r.middle[rows, :] + pair(r.x2s, r.x2r, rows) + down_bias).astype(BF)
        out_copy(k).start()
        return 0

    lax.fori_loop(0, chunks, output, 0)
    for k in range(chunks):
        out_copy(k).wait_recv()

    def out_local(k):
        rows = at(k, big)
        return local(r.hid.at[rows], r.layer_out.at[rows], LO_OUT + k)

    def unpack(k, _):
        r.hid[at(k, big), :] = unpacked(r.lo, start, n, k, big).astype(BF)
        out_local(k).start()
        return 0

    lax.fori_loop(0, s.length // big, unpack, 0)

    if s.short:
        last_stage(2)
    vec_y.wait_recv()
    r.sums_out[0:2, :] = r.vec3[0:2, :] + r.vec_y[0:2, :]
    r.sums_out[2:8, :] = r.vec3[2:8, :]

    sends = [small_copy, sums_copy, vec_y] + sib_weights + [grad_copy(kind) for kind in range(3)]
    if s.short:
        sends = sends + [vec_x] + vec_z
        for kind in range(3):
            sends = sends + [x_copy(kind, step) for step in range(zs)] + [z_copy(kind, step) for step in range(zs - 1)]
    for copy in sends:
        copy.wait_send()

    def ends(k, _):
        rows = at(k)
        for sent, landed, sem in ((r.x1s, r.x1r, X1), (r.x2s, r.x2r, X2), (r.x3s, r.x3r, X3), (r.x4s, r.x4r, X4)):
            swap(sent, landed, sem, k).wait_send()
        out_copy(k).wait_send()
        out_local(k).wait()
        block_copy(r.ig, k, IG).wait()
        local(r.ig.at[rows], r.input_grad.at[core, rows], IG_OUT + k).wait()
        return 0

    lax.fori_loop(0, chunks, ends, 0)


def unpacked(packed, start, n, k, size):
    position = lax.broadcasted_iota(jnp.int32, (size, 1), 0) + k * size
    slots = lax.broadcasted_iota(jnp.int32, (size, n), 1)
    choose = jnp.where(slots + start == position, 1.0, 0.0).astype(BF)
    inside = jnp.where(position >= start, 1.0, 0.0) * jnp.where(position < start + n, 1.0, 0.0)
    rest = packed[1, pl.ds(pl.multiple_of(lax.rem(k * size, n), size), size), :].astype(F32)
    return jnp.where(inside > 0.5, dot(choose, packed[0]), rest)


def layer_call(s, vectors, arrays):
    n, width, cols, hid = s.rows, s.width, s.head_cols, s.hidden
    zs, share, big = s.zs, s.share, 2 * s.chunk
    outputs = dict(
        layer_out=((s.length, width), BF, pl.ANY),
        input_grad=((2, n, width), BF, pl.ANY),
        grads=((3, share, hid) if s.short else (3, zs, 2, share, hid), F32 if s.short else BF, pltpu.VMEM),
        sums_out=((8, width), F32, pltpu.VMEM),
    )
    swapped = ((n, width), BF)
    rows32 = ((n, width), F32)
    blocks = ((3, zs, 2, share, hid), BF)
    table = ((8, width), F32)
    scratch = dict(
        hid=((s.length, width), BF),
        cot=((s.length, width), BF),
        wqkv=((2, 3, cols, width), BF),
        wo=((2, cols, width), BF),
        wu=((2, width, hid), BF),
        wd=((2, hid, width), BF),
        small=((16, width), F32),
        small_sib=table,
        docs=((n, 8), BF),
        bias=((n, n), F32),
        resid=rows32,
        attn_in=swapped,
        cotp=swapped,
        qkv=((2, 3, n, cols), BF),
        probs=((2 * s.heads, n, n), BF),
        mixed32=((2, n, cols), F32),
        mixed=((2, n, cols), BF),
        middle=rows32,
        mlp_in=swapped,
        act=((2, n, hid), BF),
        gpre=((2, n, hid), BF),
        pre=((big, hid), F32),
        dact=((big, hid), F32),
        gmid=rows32,
        gml=swapped,
        dk=((2, n, cols), F32),
        dv=((2, n, cols), F32),
        dqkv=((2, 3, n, cols), BF),
        t1=((width, n), BF),
        t2=((width, n), BF),
        gs=blocks,
        go=blocks,
        gr=blocks,
        sums=((16, width), F32),
        sums_r=((16, width), F32),
        vec=table,
        vec3=table,
        vec_y=table,
        x1s=swapped,
        x1r=swapped,
        x2s=swapped,
        x2r=swapped,
        x3s=swapped,
        x3r=swapped,
        x4s=swapped,
        x4r=swapped,
        lo=((2, n, width), BF),
        ig=swapped,
    )
    if s.short:
        scratch.update(
            xs=((3, zs, share, hid), BF),
            xr=((3, zs, share, hid), BF),
            zs=((3, zs - 1, share, hid), BF),
            zr=((3, zs - 1, share, hid), BF),
        )
    scratch.update(vec_r=table, vec2=table, vec_z=((zs - 1, 8, width), F32))
    for name, value in vectors.items():
        scratch["v_" + name] = (value.shape, value.dtype)
    semaphores = dict(
        local_sem=pltpu.SemaphoreType.DMA((32,)),
        send_sem=pltpu.SemaphoreType.DMA((72,)),
        recv_sem=pltpu.SemaphoreType.DMA((72,)),
    )
    names = [*vectors, *arrays, *outputs, *scratch, *semaphores]
    return pl.pallas_call(
        functools.partial(layer_kernel, s, names, list(vectors)),
        out_shape=[jax.ShapeDtypeStruct(shape, kind) for shape, kind, _ in outputs.values()],
        in_specs=[pl.BlockSpec(memory_space=pl.ANY)] * (len(vectors) + len(arrays)),
        out_specs=[pl.BlockSpec(memory_space=space) for _, _, space in outputs.values()],
        scratch_shapes=[pltpu.VMEM(shape, kind) for shape, kind in scratch.values()] + list(semaphores.values()),
        compiler_params=pltpu.CompilerParams(
            collective_id=0, has_side_effects=True, vmem_limit_bytes=VMEM_LIMIT
        ),
        name="layer",
    )(*vectors.values(), *arrays.values())


def finish_kernel(s, names, *refs):
    r = types.SimpleNamespace(**dict(zip(names, refs)))
    n, width, cols, share = s.rows, s.width, s.head_cols, s.own_share
    size = n // 2

    def copy(source, target, at):
        return pltpu.make_async_copy(source, target, r.sem.at[at])

    seg_in = copy(r.segments, r.seg, 15)
    seg_in.start()
    ig_in = copy(r.grad_in, r.packed, 0)
    ig_in.start()
    lo_in = copy(r.layer_in, r.lo, 1)
    lo_in.start()
    grads_in = [copy(r.grads.at[kind], r.held.at[kind], 2 + kind) for kind in range(3)]
    for one in grads_in:
        one.start()
    sums_in = copy(r.sums, r.table, 14)
    sums_in.start()
    seg_in.wait()
    start = longest_start(r.seg[...], s.docs)
    r.embed[...] = jnp.zeros_like(r.embed[...])
    lo_out = copy(r.lo, r.layer_out, 1)
    wd_out = copy(r.held.at[0], r.wd, 2)
    wu_out = copy(r.held.at[1], r.wu, 3)
    ig_in.wait()

    def ig_out(k):
        rows = pl.ds(pl.multiple_of(k * size, size), size)
        return copy(r.rows_out.at[rows], r.input_grad.at[rows], 8 + k)

    def unpack(k, _):
        rows = pl.ds(pl.multiple_of(k * size, size), size)
        y = unpacked(r.packed, start, n, k, size)
        r.rows_out[rows, :] = y
        ig_out(k).start()
        docs = jnp.where(lax.broadcasted_iota(jnp.int32, (8, size), 0) == r.seg[0:1, rows], 1.0, 0.0).astype(BF)
        r.embed[0] = r.embed[0] + dot(docs, y.astype(BF))[0 : s.docs]
        return 0

    unpack(0, 0)
    lo_in.wait()
    lo_out.start()
    lax.fori_loop(1, s.length // size, unpack, 0)
    grads_in[0].wait()
    wd_out.start()
    grads_in[1].wait()
    wu_out.start()
    dp_at = lax.axis_index("dp")
    sums_in.wait()
    table = pltpu.roll(r.table[...], lax.rem(width - dp_at * share, width), 1)
    for row, target in enumerate((r.fg, r.fs, r.sg, r.ss, r.ob, r.db, r.ub)):
        target[...] = table[row : row + 1, 0:share]
    small = cols // s.dp
    heads = pltpu.roll(r.table[...], lax.rem(width - dp_at * small, width), 1)
    r.qb[...] = heads[7:8, 0:small]
    r.vb[...] = heads[7:8, 256 : 256 + small]
    grads_in[2].wait()
    attn = r.held[2]
    r.wq[...] = attn[:, 0:cols]
    r.wk[...] = attn[:, cols : 2 * cols]
    r.wv[...] = attn[:, 2 * cols : 3 * cols]
    r.wo[...] = attn[:, 3 * cols : 4 * cols].T
    lo_out.wait()
    wd_out.wait()
    wu_out.wait()
    for k in range(s.length // size):
        ig_out(k).wait()


def finish_call(s, segments, layer_in, grad_in, grads, sums):
    width, share, cols, hid = s.width, s.own_share, s.head_cols, s.hidden
    small = cols // s.dp
    arrays = dict(segments=segments, layer_in=layer_in, grad_in=grad_in, grads=grads, sums=sums)
    outputs = dict(
        layer_out=(s.length, width),
        input_grad=(s.length, width),
        embed=(1, s.docs, width),
        fg=(1, share),
        fs=(1, share),
        wq=(share, cols),
        qb=(1, small),
        wk=(share, cols),
        wv=(share, cols),
        vb=(1, small),
        wo=(cols, share),
        ob=(1, share),
        sg=(1, share),
        ss=(1, share),
        wu=(share, hid),
        ub=(1, share),
        wd=(share, hid),
        db=(1, share),
    )
    far = ("layer_out", "input_grad", "wu", "wd")
    scratch = dict(
        seg=(segments.shape, segments.dtype),
        packed=(grad_in.shape, BF),
        lo=(layer_in.shape, BF),
        rows_out=((s.length, width), F32),
        held=(grads.shape, F32),
        table=(sums.shape, F32),
    )
    names = [*arrays, *outputs, *scratch, "sem"]
    return pl.pallas_call(
        functools.partial(finish_kernel, s, names),
        out_shape=[
            jax.ShapeDtypeStruct(shape, BF if name == "layer_out" else F32) for name, shape in outputs.items()
        ],
        in_specs=[pl.BlockSpec(memory_space=pl.ANY)] * len(arrays),
        out_specs=[pl.BlockSpec(memory_space=pl.ANY if name in far else pltpu.VMEM) for name in outputs],
        scratch_shapes=[pltpu.VMEM(shape, kind) for shape, kind in scratch.values()]
        + [pltpu.SemaphoreType.DMA((16,))],
        compiler_params=pltpu.CompilerParams(vmem_limit_bytes=VMEM_LIMIT),
        name="finish",
    )(*arrays.values())


def on_device(
    dp,
    hidden_in,
    document_time_vectors,
    segment_ids,
    first_gain,
    first_shift,
    query_weight,
    query_bias,
    key_weight,
    value_weight,
    value_bias,
    out_weight,
    out_bias,
    second_gain,
    second_shift,
    up_weight,
    up_bias,
    down_weight,
    down_bias,
    cotangent,
):
    length, width = hidden_in.shape
    cols, hidden = query_weight.shape[1], up_weight.shape[1]
    s = Shape(length, width, cols, hidden, document_time_vectors.shape[1], dp)

    vectors = dict(
        segments=segment_ids,
        doc_vectors=document_time_vectors,
        first_gain=first_gain,
        first_shift=first_shift,
        second_gain=second_gain,
        second_shift=second_shift,
        out_bias=out_bias,
        down_bias=down_bias,
        up_bias=up_bias,
        query_bias=query_bias,
        value_bias=value_bias,
    )
    arrays = dict(
        hidden=hidden_in,
        cotangent=cotangent,
        query=query_weight.T,
        key=key_weight.T,
        value=value_weight.T,
        out=out_weight,
        up=up_weight,
        down=down_weight,
    )
    layer_out, input_grad, grads, sums = layer_call(s, vectors, arrays)
    if not s.short:
        grads = grads.reshape(3, width, width)
        grads = lax.psum_scatter(grads, "dp", scatter_dimension=1, tiled=True).astype(F32)
        sums = lax.psum(sums, "dp")
    results = finish_call(s, segment_ids, layer_out, input_grad, grads, sums)
    results = [y.reshape(y.shape[1]) if y.ndim == 2 and y.shape[0] == 1 else y for y in results]
    results[16] = results[16].T
    return tuple(results)


def solution(mesh):
    placed = (
        P("dp", None),
        P("dp", None, None),
        P("dp", None),
        P(),
        P(),
        P(None, "tensor"),
        P("tensor"),
        P(None, "tensor"),
        P(None, "tensor"),
        P("tensor"),
        P("tensor", None),
        P(),
        P(),
        P(),
        P(None, "tensor"),
        P("tensor"),
        P("tensor", None),
        P(),
        P("dp", None),
    )
    return jax.shard_map(
        functools.partial(on_device, mesh.shape["dp"]),
        mesh=mesh,
        in_specs=placed,
        out_specs=(
            P("dp", None),
            P("dp", None),
            P("dp", None, None),
            P("dp"),
            P("dp"),
            P("dp", "tensor"),
            P(("tensor", "dp")),
            P("dp", "tensor"),
            P("dp", "tensor"),
            P(("tensor", "dp")),
            P("tensor", "dp"),
            P("dp"),
            P("dp"),
            P("dp"),
            P("dp", "tensor"),
            P(("tensor", "dp")),
            P("tensor", "dp"),
            P("dp"),
        ),
        check_vma=False,
    )
```

```python
import functools
import math
import types

import jax
import jax.numpy as jnp
from jax import lax
from jax.experimental import pallas as pl
from jax.experimental.pallas import tpu as pltpu
from jax.sharding import PartitionSpec as P

DH = 64
EPSILON = 1e-05
MASKED = -1000000000.0
BF = jnp.bfloat16
F32 = jnp.float32
MESH = pl.DeviceIdType.MESH
VMEM_LIMIT = 67_000_000


def dot(left, right, left_dim=1, right_dim=0):
    return lax.dot_general(
        left, right, (((left_dim,), (right_dim,)), ((), ())), preferred_element_type=F32
    )


def normalize(rows):
    average = jnp.mean(rows, axis=-1, keepdims=True)
    centered = rows - average
    variance = jnp.mean(centered * centered, axis=-1, keepdims=True)
    scale = lax.rsqrt(variance + EPSILON)
    return centered * scale, scale


def norm_back(normal, scale, gain, grad):
    inner = grad * gain
    first = jnp.mean(inner, axis=-1, keepdims=True)
    second = jnp.mean(inner * normal, axis=-1, keepdims=True)
    return scale * (inner - first - normal * second)


def packed_source(slots, start, half, block):
    return (1 - block) * (slots + start) + block * (slots + jnp.where(slots >= start, half, 0))


def longest_start(segments, docs):
    half = segments.shape[1] // 2
    longest = jnp.zeros((1, 1), F32)
    for doc in range(docs):
        count = jnp.sum(jnp.where(segments == doc, 1.0, 0.0), axis=1, keepdims=True)
        longest = longest + jnp.where(count == half, float(doc), 0.0)
    before = jnp.where(segments.astype(F32) < longest, 1.0, 0.0)
    return jnp.sum(before, axis=1, keepdims=True).astype(jnp.int32)


class Shape:
    def __init__(self, length, width, head_cols, hidden, docs, dp):
        self.length, self.width, self.head_cols, self.hidden = length, width, head_cols, hidden
        self.docs, self.dp = docs, dp
        self.rows = length // 2
        self.short = 4 <= dp <= 8 and width // dp % 16 == 0
        blocks = dp if self.short else 8
        self.zs = blocks // 2
        self.share = width // blocks
        self.own_share = width // dp
        self.chunk = self.rows // 4
        self.chunks = 4
        self.heads = head_cols // DH


def layer_kernel(s, names, small_names, *refs):
    r = types.SimpleNamespace(**dict(zip(names, refs)))
    width, n, cols, hidden = s.width, s.rows, s.head_cols, s.hidden
    zs, share, chunk, chunks = s.zs, s.share, s.chunk, s.chunks
    big = 2 * chunk
    dp_at, tensor_at = lax.axis_index("dp"), lax.axis_index("tensor")
    core, side = lax.rem(tensor_at, 2), lax.div(tensor_at, 2)
    x_at, z_at = lax.rem(dp_at, 2), lax.div(dp_at, 2)
    sibling = (dp_at, side * 2 + 1 - core)
    peer = (dp_at, (1 - side) * 2 + core)
    across = (z_at * 2 + 1 - x_at, tensor_at)

    def along(step):
        return (lax.rem(z_at + step, zs) * 2 + x_at, tensor_at)

    def local(source, target, at):
        return pltpu.make_async_copy(source, target, r.local_sem.at[at])

    def remote(source, target, at, device):
        return pltpu.make_async_remote_copy(
            src_ref=source,
            dst_ref=target,
            send_sem=r.send_sem.at[at],
            recv_sem=r.recv_sem.at[at],
            device_id=device,
            device_id_type=MESH,
        )

    WEIGHTS, X1, X2, X3, X4, GRADS, XS, ZS, SUMS, LO, IG = 0, 8, 12, 16, 20, 24, 28, 40, 52, 60, 64
    SMALL, LO_OUT, IG_OUT, GRADS_OUT = 8, 20, 24, 28

    barrier = pltpu.get_barrier_semaphore()
    partners = [sibling, peer]
    if s.short:
        partners = partners + [across] + [along(step) for step in range(1, zs)]
    for partner in partners:
        pl.semaphore_signal(barrier, inc=1, device_id=partner, device_id_type=MESH)

    weights = [
        (r.query, r.wqkv.at[:, 0]),
        (r.key, r.wqkv.at[:, 1]),
        (r.value, r.wqkv.at[:, 2]),
        (r.out, r.wo),
        (r.up, r.wu),
        (r.down, r.wd),
    ]
    small_copies = [
        local(getattr(r, name), getattr(r, "v_" + name), SMALL + i) for i, name in enumerate(small_names)
    ]
    for copy in small_copies:
        copy.start()
    local_hidden = local(r.hidden, r.hid, 0)
    local_hidden.start()
    own_weights = [local(src, dst.at[0], 2 + i) for i, (src, dst) in enumerate(weights)]
    for copy in own_weights[:4]:
        copy.start()
    local_cot = local(r.cotangent, r.cot, 1)
    local_cot.start()
    for copy in own_weights[4:]:
        copy.start()
    for copy in small_copies:
        copy.wait()
    small = r.small
    first_rows = (r.v_first_gain, r.v_first_shift, r.v_second_gain, r.v_second_shift, r.v_out_bias, r.v_down_bias)
    for row, ref in enumerate(first_rows + (None, None, r.v_up_bias, r.v_query_bias, r.v_value_bias)):
        if ref is not None:
            count = ref.shape[0]
            small[row : row + 1, 0:count] = ref[...].reshape(1, count).astype(F32)
    gain_one, shift_one = small[0:1, :], small[1:2, :]
    gain_two, shift_two = small[2:3, :], small[3:4, :]
    out_bias, down_bias = small[4:5, :], small[5:6, :]
    segments = r.v_segments[...]
    start = longest_start(segments, s.docs)
    doc_row = lax.broadcasted_iota(jnp.int32, (8, s.length), 0)
    docs_full = jnp.where(segments == doc_row, 1.0, 0.0).astype(BF)
    doc_vectors = r.v_doc_vectors[0]

    pl.semaphore_wait(barrier, len(partners))
    small_copy = remote(r.small.at[pl.ds(8, 8)], r.small_sib, WEIGHTS + 6, sibling)
    small_copy.start()
    sib_weights = [remote(src, dst.at[1], WEIGHTS + i, sibling) for i, (src, dst) in enumerate(weights)]
    for copy in sib_weights:
        copy.start()

    def at(k, size=chunk):
        return pl.ds(pl.multiple_of(k * size, size), size)

    def choice(k):
        slots = lax.broadcasted_iota(jnp.int32, (big, 1), 0) + k * big
        source = packed_source(slots, start, n, core)
        columns = lax.broadcasted_iota(jnp.int32, (big, s.length), 1)
        return jnp.where(columns == source, 1.0, 0.0).astype(BF)

    local_hidden.wait()
    for copy in own_weights[:3]:
        copy.wait()

    def projections(half, rows, source):
        for j in range(3):
            y = dot(source, r.wqkv[half, j], 1, 1)
            if j != 1:
                bias_row = small if half == 0 else r.small_sib
                base = 8 if half == 0 else 0
                y = y + bias_row[base + 1 + j // 2 : base + 2 + j // 2, 0:cols]
            r.qkv[half, j, rows, :] = y.astype(BF)

    def pack(k, _):
        rows = at(k, big)
        choose = choice(k)
        docs_here = dot(choose, docs_full, 1, 1).astype(BF)
        r.docs[rows, :] = docs_here
        x = dot(choose, r.hid[...]) + dot(docs_here[:, 0 : s.docs], doc_vectors)
        r.resid[rows, :] = x
        normal, _ = normalize(x)
        y = (normal * gain_one + shift_one).astype(BF)
        r.attn_in[rows, :] = y
        projections(0, rows, y)
        return 0

    lax.fori_loop(0, n // big, pack, 0, unroll=True)
    docs_all = r.docs[...]

    small_copy.wait_recv()
    for copy in sib_weights[:3]:
        copy.wait_recv()

    def second_half(k, _):
        rows = at(k, big)
        r.bias[rows, :] = (dot(r.docs[rows, :], docs_all, 1, 1) - 1.0) * (-MASKED)
        projections(1, rows, r.attn_in[rows, :])
        return 0

    lax.fori_loop(0, n // big, second_half, 0, unroll=True)
    own_weights[3].wait()
    sib_weights[3].wait_recv()

    lane = lax.broadcasted_iota(jnp.int32, (1, 128), 1)
    low = jnp.where(lane < DH, 1.0, 0.0)
    high = 1.0 - low
    factor = 1.0 / math.sqrt(DH)
    groups = [(0, 128, (low, high)), (128, 192, (None,))]

    def masked(values, mask, scale=1.0):
        if mask is None:
            return values if scale == 1.0 else values * jnp.asarray(scale, BF)
        return values * (mask * scale).astype(BF)

    def swap(sent, landed, sem, k):
        rows = at(k)
        return remote(sent.at[rows], landed.at[rows], sem + k, peer)

    def forward(k, _):
        rows = at(k)
        bias = r.bias[rows, :]
        for half in range(2):
            for first, last, masks in groups:
                q = r.qkv[half, 0, rows, first:last]
                keys = r.qkv[half, 1, :, first:last]
                values = r.qkv[half, 2, :, first:last]
                mixed = None
                for j, mask in enumerate(masks):
                    head = half * s.heads + first // DH + j
                    scores = dot(masked(q, mask, factor), keys, 1, 1) + bias
                    top = jnp.max(scores, axis=1, keepdims=True)
                    e = jnp.exp(scores - top)
                    total = jnp.sum(e, axis=1, keepdims=True)
                    probs = (e * (1.0 / total)).astype(BF)
                    r.probs[head, rows, :] = probs
                    part = dot(probs, masked(values, mask))
                    mixed = part if mixed is None else mixed + part
                r.mixed32[half, rows, first:last] = mixed
                r.mixed[half, rows, first:last] = mixed.astype(BF)
        partial = dot(r.mixed[0, rows, :], r.wo[0]) + dot(r.mixed[1, rows, :], r.wo[1])
        r.x1s[rows, :] = partial.astype(BF)
        swap(r.x1s, r.x1r, X1, k).start()
        return 0

    lax.fori_loop(0, chunks, forward, 0)

    local_cot.wait()

    def pack_cotangent(k, _):
        r.cotp[at(k, big), :] = dot(choice(k), r.cot[...]).astype(BF)
        return 0

    lax.fori_loop(0, n // big, pack_cotangent, 0)
    r.t2[...] = r.cotp[...].T

    for copy in own_weights[4:]:
        copy.wait()
    for copy in sib_weights[4:]:
        copy.wait_recv()
    up_bias = (small[8:9, :], r.small_sib[0:1, :])
    r.sums[...] = jnp.zeros_like(r.sums[...])

    def add_sum(row, values):
        count = values.shape[1]
        r.sums[row : row + 1, 0:count] = r.sums[row : row + 1, 0:count] + jnp.sum(values, axis=0, keepdims=True)

    def pair(sent, landed, rows):
        return sent[rows, :].astype(F32) + landed[rows, :].astype(F32)

    def grad_copy(kind):
        return remote(r.gs.at[kind], r.gr.at[kind], GRADS + kind, sibling)

    def block_grad(kind, left, right, target):
        for part in range(2):
            top = part * (width // 2)
            y = dot(left[top : top + width // 2, :], right)
            target[kind, part * (zs // 2) : (part + 1) * (zs // 2)] = y.astype(BF).reshape(zs // 2, 2, share, hidden)

    def mlp(k, _):
        rows = at(k, big)
        for i in range(2):
            swap(r.x1s, r.x1r, X1, 2 * k + i).wait_recv()
        middle = r.resid[rows, :] + pair(r.x1s, r.x1r, rows) + out_bias
        r.middle[rows, :] = middle
        normal, _ = normalize(middle)
        source = (normal * gain_two + shift_two).astype(BF)
        r.mlp_in[rows, :] = source
        grad_top = r.cotp[rows, :]
        add_sum(5, grad_top.astype(F32))
        grad_in = jnp.zeros((big, width), F32)
        for half in range(2):
            r.pre[...] = dot(source, r.wu[half]) + up_bias[half]
            r.dact[...] = dot(grad_top, r.wd[half], 1, 1)

            def gelu(i, _):
                part = pl.ds(pl.multiple_of(i * 16, 16), 16)
                v = r.pre[part, :]
                cdf = 0.5 * (1.0 + lax.erf(v * math.sqrt(0.5)))
                pdf = jnp.exp(-0.5 * v * v) * (1.0 / math.sqrt(2.0 * math.pi))
                where = pl.ds(pl.multiple_of(k * big + i * 16, 16), 16)
                r.act[half, where, :] = (v * cdf).astype(BF)
                r.gpre[half, where, :] = (r.dact[part, :] * (cdf + v * pdf)).astype(BF)
                return 0

            lax.fori_loop(0, big // 16, gelu, 0)

        @pl.when(k == n // big - 1)
        def _():
            block_grad(0, r.t2, r.act[1], r.gs)
            grad_copy(0).start()

        for half in range(2):
            grad_pre = r.gpre[half, rows, :]
            add_sum(6 + 2 * half, grad_pre.astype(F32))
            grad_in = grad_in + dot(grad_pre, r.wu[half], 1, 1)
        r.x3s[rows, :] = grad_in.astype(BF)
        for i in range(2):
            swap(r.x3s, r.x3r, X3, 2 * k + i).start()
        return 0

    lax.fori_loop(0, n // big, mlp, 0)

    block_grad(0, r.t2, r.act[0], r.go)
    r.t1[...] = r.mlp_in[...].T
    block_grad(1, r.t1, r.gpre[1], r.gs)
    grad_copy(1).start()

    def both(kind, z, which):
        return r.go[kind, z, which].astype(F32) + r.gr[kind, z, which].astype(F32)

    def x_copy(kind, step):
        z = lax.rem(z_at + 1 + step, zs)
        return remote(r.xs.at[kind, z], r.xr.at[kind, z], XS + kind * zs + step, across)

    def z_copy(kind, step):
        return remote(r.zs.at[kind, step], r.zr.at[kind, step], ZS + kind * (zs - 1) + step, along(step + 1))

    def x_stage(kind):
        grad_copy(kind).wait_recv()
        for step in range(zs):
            z = lax.rem(z_at + 1 + step, zs)
            r.xs[kind, z] = both(kind, z, 1 - x_at).astype(BF)
            x_copy(kind, step).start()

    def x_sum(kind, step):
        z = lax.rem(z_at + 1 + step, zs)
        x_copy(kind, step).wait_recv()
        return both(kind, z, x_at) + r.xr[kind, z].astype(F32)

    def z_step(kind, step):
        r.zs[kind, step] = x_sum(kind, step).astype(BF)
        z_copy(kind, step).start()

    def z_stage(kind, first=0):
        for step in range(first, zs - 1):
            z_step(kind, step)
        r.total[kind] = x_sum(kind, zs - 1)

    def grad_out(kind):
        return local(r.total.at[kind], r.grads.at[kind], GRADS_OUT + kind)

    def last_stage(kind):
        y = r.total[kind]
        for step in range(zs - 1):
            z_copy(kind, step).wait_recv()
            y = y + r.zr[kind, step].astype(F32)
        r.total[kind] = y
        grad_out(kind).start()

    def whole_sum(kind):
        grad_copy(kind).wait_recv()
        r.total[kind] = (r.go[kind].astype(F32) + r.gr[kind].astype(F32)).astype(BF)
        grad_out(kind).start()

    for kind in range(2):
        if kind == 1:
            block_grad(1, r.t1, r.gpre[0], r.go)
        if s.short:
            x_stage(kind)
        else:
            whole_sum(kind)

    def mlp_out(k, _):
        rows = at(k, big)
        part = dot(r.act[0, rows, :], r.wd[0]) + dot(r.act[1, rows, :], r.wd[1])
        r.x2s[rows, :] = part.astype(BF)
        return 0

    lax.fori_loop(0, n // big, mlp_out, 0)
    for k in range(2):
        swap(r.x2s, r.x2r, X2, k).start()

    r.dk[...] = jnp.zeros_like(r.dk[...])
    r.dv[...] = jnp.zeros_like(r.dv[...])

    def backward(k, _):
        rows = at(k)
        swap(r.x3s, r.x3r, X3, k).wait_recv()
        grad_in = pair(r.x3s, r.x3r, rows)
        normal, scale = normalize(r.middle[rows, :])
        add_sum(2, grad_in * normal)
        add_sum(3, grad_in)
        grad_middle = r.cotp[rows, :].astype(F32) + norm_back(normal, scale, gain_two, grad_in)
        r.gmid[rows, :] = grad_middle
        grad_low = grad_middle.astype(BF)
        r.gml[rows, :] = grad_low
        add_sum(4, grad_low.astype(F32))
        for half in range(2):
            grad_mixed = dot(grad_low, r.wo[half], 1, 1).astype(BF)
            for first, last, masks in groups:
                q = r.qkv[half, 0, rows, first:last]
                keys = r.qkv[half, 1, :, first:last]
                values = r.qkv[half, 2, :, first:last]
                out = grad_mixed[:, first:last]
                product = out.astype(F32) * r.mixed32[half, rows, first:last]
                dq = dk = dv = None
                for j, mask in enumerate(masks):
                    head = half * s.heads + first // DH + j
                    inner = jnp.sum(product if mask is None else product * mask, axis=1, keepdims=True)
                    own_out = masked(out, mask)
                    probs = r.probs[head, rows, :]
                    grad_probs = dot(own_out, values, 1, 1)
                    grad_scores = (probs.astype(F32) * (grad_probs - inner)).astype(BF)
                    parts = (
                        dot(grad_scores, masked(keys, mask, factor)),
                        dot(grad_scores, masked(q, mask, factor), 0, 0),
                        dot(probs, own_out, 0, 0),
                    )
                    if dq is None:
                        dq, dk, dv = parts
                    else:
                        dq, dk, dv = dq + parts[0], dk + parts[1], dv + parts[2]
                r.dqkv[half, 0, rows, first:last] = dq.astype(BF)
                r.dk[half, :, first:last] = r.dk[half, :, first:last] + dk
                r.dv[half, :, first:last] = r.dv[half, :, first:last] + dv
        if s.short:

            @pl.when(k < zs - 1)
            def _():
                z_step(0, k)

        return 0

    lax.fori_loop(0, chunks, backward, 0)
    r.dqkv[:, 1] = r.dk[...].astype(BF)
    r.dqkv[:, 2] = r.dv[...].astype(BF)

    def attn_in_grad(k, _):
        rows = at(k, big)
        part = jnp.zeros((big, width), F32)
        for half in range(2):
            for j in range(3):
                part = part + dot(r.dqkv[half, j, rows, :], r.wqkv[half, j])
        part = part.astype(BF)
        r.x4s[rows, :] = part
        for i in range(2):
            swap(r.x4s, r.x1r, X4, 2 * k + i).start()
        normal, _ = normalize(r.resid[rows, :])
        add_sum(0, part.astype(F32) * normal)
        add_sum(1, part.astype(F32))
        return 0

    lax.fori_loop(0, n // big, attn_in_grad, 0)
    for k in range(2, chunks):
        swap(r.x2s, r.x2r, X2, k).start()

    for half in range(2):
        add_sum(7 + 2 * half, r.dqkv[half, 0].astype(F32))
        add_sum(10 + half, r.dqkv[half, 2].astype(F32))
    sums_copy = remote(r.sums, r.sums_r, SUMS, sibling)
    sums_copy.start()
    r.t1[...] = r.attn_in[...].T
    r.t2[...] = r.gml[...].T

    def attn_grads(half, target):
        for j in range(4):
            y = dot(r.t1[...], r.dqkv[half, j]) if j < 3 else dot(r.t2[...], r.mixed[half])
            target[2, :, :, :, j * cols : (j + 1) * cols] = y.astype(BF).reshape(zs, 2, share, cols)

    attn_grads(1, r.gs)
    grad_copy(2).start()
    if s.short:
        z_stage(0, zs - 1)
        z_step(1, 0)
    attn_grads(0, r.go)

    sums_copy.wait_recv()
    mine, other = r.sums, r.sums_r
    r.vec[0:6, :] = mine[0:6, :] + other[0:6, :]
    r.vec[6:7, :] = mine[6:7, :] + other[8:9, :]
    r.vec[7:8, :] = jnp.zeros((1, width), F32)
    r.vec[7:8, 0:cols] = mine[7:8, 0:cols] + other[9:10, 0:cols]
    r.vec[7:8, 256 : 256 + cols] = mine[10:11, 0:cols] + other[11:12, 0:cols]
    vec_x = remote(r.vec, r.vec_r, SUMS + 1, across)
    if s.short:
        vec_x.start()
        x_stage(2)
        z_stage(1, 1)
    else:
        whole_sum(2)

    def to_sibling(ref, k, sem):
        rows = at(k)
        return remote(ref.at[core, rows], ref.at[core, rows], sem + k, sibling)

    def input_grad(k, _):
        rows = at(k)
        swap(r.x4s, r.x1r, X4, k).wait_recv()
        grad_in = pair(r.x4s, r.x1r, rows)
        normal, scale = normalize(r.resid[rows, :])
        y = r.gmid[rows, :] + norm_back(normal, scale, gain_one, grad_in)
        r.ig[core, rows, :] = y.astype(BF)
        to_sibling(r.ig, k, IG).start()
        if s.short:

            @pl.when(k == 2)
            def _():
                z_step(2, 0)

        return 0

    lax.fori_loop(0, chunks, input_grad, 0)

    blocks = s.length // big

    def rows_out(source, target, k, sem):
        rows = at(k, big)
        return local(source.at[rows], target.at[rows], sem + k)

    def unpack_grad(k):
        y = unpacked(r.ig, start, n, k, big).astype(BF)
        r.ig_rows[at(k, big), :] = y
        rows_out(r.ig_rows, r.input_grad, k, IG_OUT).start()
        r.embed[0] = r.embed[0] + dot(docs_full[:, k * big : (k + 1) * big], y)[0 : s.docs]

    r.embed[...] = jnp.zeros_like(r.embed[...])
    vec_z = [remote(r.vec2, r.vec_z.at[step], SUMS + 2 + step, along(step + 1)) for step in range(zs - 1)]
    if s.short:
        vec_x.wait_recv()
        r.vec2[...] = r.vec[...] + r.vec_r[...]
        for copy in vec_z:
            copy.start()
    if s.short:
        z_stage(2, 1)
    for k in range(chunks):
        to_sibling(r.ig, k, IG).wait_recv()
    for k in range(blocks):
        unpack_grad(k)
    if s.short:
        last_stage(0)
        table = r.vec2[...]
        for step, copy in enumerate(vec_z):
            copy.wait_recv()
            table = table + r.vec_z[step]
        r.vec3[...] = table
        last_stage(1)
    else:
        r.vec3[...] = r.vec[...]
    vec_y = remote(r.vec3, r.vec_y, SUMS + 2 + zs, peer)
    vec_y.start()

    def output(k, _):
        rows = at(k)
        swap(r.x2s, r.x2r, X2, k).wait_recv()
        r.lo[core, rows, :] = (r.middle[rows, :] + pair(r.x2s, r.x2r, rows) + down_bias).astype(BF)
        to_sibling(r.lo, k, LO).start()
        return 0

    lax.fori_loop(0, chunks, output, 0)
    for k in range(chunks):
        to_sibling(r.lo, k, LO).wait_recv()

    def unpack(k, _):
        r.hid[at(k, big), :] = unpacked(r.lo, start, n, k, big).astype(BF)
        rows_out(r.hid, r.layer_out, k, LO_OUT).start()
        return 0

    lax.fori_loop(0, blocks, unpack, 0)

    if s.short:
        last_stage(2)
    vec_y.wait_recv()
    r.sums_out[0:2, :] = r.vec3[0:2, :] + r.vec_y[0:2, :]
    r.sums_out[2:8, :] = r.vec3[2:8, :]

    sends = [small_copy, sums_copy, vec_y] + sib_weights + [grad_copy(kind) for kind in range(3)]
    if s.short:
        sends = sends + [vec_x] + vec_z
        for kind in range(3):
            sends = sends + [x_copy(kind, step) for step in range(zs)] + [z_copy(kind, step) for step in range(zs - 1)]
    for copy in sends:
        copy.wait_send()

    def ends(k, _):
        for sent, landed, sem in ((r.x1s, r.x1r, X1), (r.x2s, r.x2r, X2), (r.x3s, r.x3r, X3), (r.x4s, r.x1r, X4)):
            swap(sent, landed, sem, k).wait_send()
        to_sibling(r.lo, k, LO).wait_send()
        to_sibling(r.ig, k, IG).wait_send()
        return 0

    lax.fori_loop(0, chunks, ends, 0)
    for kind in range(3):
        grad_out(kind).wait()
    for k in range(blocks):
        rows_out(r.ig_rows, r.input_grad, k, IG_OUT).wait()
        rows_out(r.hid, r.layer_out, k, LO_OUT).wait()


def unpacked(packed, start, n, k, size):
    position = lax.broadcasted_iota(jnp.int32, (size, 1), 0) + k * size
    slots = lax.broadcasted_iota(jnp.int32, (size, n), 1)
    choose = jnp.where(slots + start == position, 1.0, 0.0).astype(BF)
    inside = jnp.where(position >= start, 1.0, 0.0) * jnp.where(position < start + n, 1.0, 0.0)
    rest = packed[1, pl.ds(pl.multiple_of(lax.rem(k * size, n), size), size), :].astype(F32)
    return jnp.where(inside > 0.5, dot(choose, packed[0]), rest)


def layer_call(s, vectors, arrays):
    n, width, cols, hid = s.rows, s.width, s.head_cols, s.hidden
    zs, share, big = s.zs, s.share, 2 * s.chunk
    total = ((3, share, hid), F32) if s.short else ((3, zs, 2, share, hid), BF)
    outputs = dict(
        layer_out=((s.length, width), BF, pl.ANY),
        input_grad=((s.length, width), BF, pl.ANY),
        embed=((1, s.docs, width), F32, pltpu.VMEM),
        grads=(*total, pl.ANY),
        sums_out=((8, width), F32, pltpu.VMEM),
    )
    swapped = ((n, width), BF)
    rows32 = ((n, width), F32)
    blocks = ((3, zs, 2, share, hid), BF)
    table = ((8, width), F32)
    scratch = dict(
        total=total,
        hid=((s.length, width), BF),
        cot=((s.length, width), BF),
        wqkv=((2, 3, cols, width), BF),
        wo=((2, cols, width), BF),
        wu=((2, width, hid), BF),
        wd=((2, hid, width), BF),
        small=((16, width), F32),
        small_sib=table,
        docs=((n, 8), BF),
        bias=((n, n), F32),
        resid=rows32,
        attn_in=swapped,
        cotp=swapped,
        qkv=((2, 3, n, cols), BF),
        probs=((2 * s.heads, n, n), BF),
        mixed32=((2, n, cols), F32),
        mixed=((2, n, cols), BF),
        middle=rows32,
        mlp_in=swapped,
        act=((2, n, hid), BF),
        gpre=((2, n, hid), BF),
        pre=((big, hid), F32),
        dact=((big, hid), F32),
        gmid=rows32,
        gml=swapped,
        dk=((2, n, cols), F32),
        dv=((2, n, cols), F32),
        dqkv=((2, 3, n, cols), BF),
        t1=((width, n), BF),
        t2=((width, n), BF),
        gs=blocks,
        go=blocks,
        gr=blocks,
        sums=((16, width), F32),
        sums_r=((16, width), F32),
        vec=table,
        vec3=table,
        vec_y=table,
        x1s=swapped,
        x1r=swapped,
        x2s=swapped,
        x2r=swapped,
        x3s=swapped,
        x3r=swapped,
        x4s=swapped,
        lo=((2, n, width), BF),
        ig=((2, n, width), BF),
        ig_rows=((s.length, width), BF),
    )
    if s.short:
        scratch.update(
            xs=((3, zs, share, hid), BF),
            xr=((3, zs, share, hid), BF),
            zs=((3, zs - 1, share, hid), BF),
            zr=((3, zs - 1, share, hid), BF),
        )
    scratch.update(vec_r=table, vec2=table, vec_z=((zs - 1, 8, width), F32))
    for name, value in vectors.items():
        scratch["v_" + name] = (value.shape, value.dtype)
    semaphores = dict(
        local_sem=pltpu.SemaphoreType.DMA((32,)),
        send_sem=pltpu.SemaphoreType.DMA((72,)),
        recv_sem=pltpu.SemaphoreType.DMA((72,)),
    )
    names = [*vectors, *arrays, *outputs, *scratch, *semaphores]
    return pl.pallas_call(
        functools.partial(layer_kernel, s, names, list(vectors)),
        out_shape=[jax.ShapeDtypeStruct(shape, kind) for shape, kind, _ in outputs.values()],
        in_specs=[pl.BlockSpec(memory_space=pl.ANY)] * (len(vectors) + len(arrays)),
        out_specs=[pl.BlockSpec(memory_space=space) for _, _, space in outputs.values()],
        scratch_shapes=[pltpu.VMEM(shape, kind) for shape, kind in scratch.values()] + list(semaphores.values()),
        compiler_params=pltpu.CompilerParams(
            collective_id=0, has_side_effects=True, vmem_limit_bytes=VMEM_LIMIT
        ),
        name="layer",
    )(*vectors.values(), *arrays.values())


def finish_kernel(s, names, *refs):
    r = types.SimpleNamespace(**dict(zip(names, refs)))
    width, cols, share = s.width, s.head_cols, s.own_share
    blocks = 4
    size = s.length // blocks

    def copy(source, target, at):
        return pltpu.make_async_copy(source, target, r.sem.at[at])

    def rows(k):
        return pl.ds(k * size, size)

    ig_in = [copy(r.grad_in.at[rows(k)], r.held_grad.at[rows(k)], 16 + k) for k in range(blocks)]
    ig_out = [copy(r.rows_out.at[rows(k)], r.input_grad.at[rows(k)], 8 + k) for k in range(blocks)]
    for one in ig_in:
        one.start()
    lo_in = copy(r.layer_in, r.lo, 1)
    lo_in.start()
    grads_in = [copy(r.grads.at[kind], r.held.at[kind], 2 + kind) for kind in range(3)]
    for one in grads_in:
        one.start()
    sums_in = copy(r.sums, r.table, 14)
    sums_in.start()
    embed_in = copy(r.embed_in, r.embed, 15)
    embed_in.start()
    lo_out = copy(r.lo, r.layer_out, 1)
    wd_out = copy(r.held.at[0], r.wd, 2)
    wu_out = copy(r.held.at[1], r.wu, 3)
    for k in range(blocks):
        ig_in[k].wait()
        r.rows_out[rows(k), :] = r.held_grad[rows(k), :].astype(F32)
        ig_out[k].start()
    lo_in.wait()
    lo_out.start()
    grads_in[0].wait()
    wd_out.start()
    grads_in[1].wait()
    wu_out.start()
    dp_at = lax.axis_index("dp")
    sums_in.wait()
    table = pltpu.roll(r.table[...], lax.rem(width - dp_at * share, width), 1)
    for row, target in enumerate((r.fg, r.fs, r.sg, r.ss, r.ob, r.db, r.ub)):
        target[...] = table[row : row + 1, 0:share]
    small = cols // s.dp
    heads = pltpu.roll(r.table[...], lax.rem(width - dp_at * small, width), 1)
    r.qb[...] = heads[7:8, 0:small]
    r.vb[...] = heads[7:8, 256 : 256 + small]
    grads_in[2].wait()
    attn = r.held[2]
    r.wq[...] = attn[:, 0:cols]
    r.wk[...] = attn[:, cols : 2 * cols]
    r.wv[...] = attn[:, 2 * cols : 3 * cols]
    r.wo[...] = attn[:, 3 * cols : 4 * cols].T
    lo_out.wait()
    wd_out.wait()
    wu_out.wait()
    embed_in.wait()
    for one in ig_out:
        one.wait()


def finish_call(s, layer_in, grad_in, embed_in, grads, sums):
    width, share, cols, hid = s.width, s.own_share, s.head_cols, s.hidden
    small = cols // s.dp
    arrays = dict(layer_in=layer_in, grad_in=grad_in, embed_in=embed_in, grads=grads, sums=sums)
    outputs = dict(
        layer_out=(s.length, width),
        input_grad=(s.length, width),
        embed=(1, s.docs, width),
        fg=(1, share),
        fs=(1, share),
        wq=(share, cols),
        qb=(1, small),
        wk=(share, cols),
        wv=(share, cols),
        vb=(1, small),
        wo=(cols, share),
        ob=(1, share),
        sg=(1, share),
        ss=(1, share),
        wu=(share, hid),
        ub=(1, share),
        wd=(share, hid),
        db=(1, share),
    )
    far = ("layer_out", "input_grad", "wu", "wd")
    scratch = dict(
        held_grad=(grad_in.shape, BF),
        lo=(layer_in.shape, BF),
        rows_out=((s.length, width), F32),
        held=(grads.shape, F32),
        table=(sums.shape, F32),
    )
    names = [*arrays, *outputs, *scratch, "sem"]
    return pl.pallas_call(
        functools.partial(finish_kernel, s, names),
        out_shape=[
            jax.ShapeDtypeStruct(shape, BF if name == "layer_out" else F32) for name, shape in outputs.items()
        ],
        in_specs=[pl.BlockSpec(memory_space=pl.ANY)] * len(arrays),
        out_specs=[pl.BlockSpec(memory_space=pl.ANY if name in far else pltpu.VMEM) for name in outputs],
        scratch_shapes=[pltpu.VMEM(shape, kind) for shape, kind in scratch.values()]
        + [pltpu.SemaphoreType.DMA((20,))],
        compiler_params=pltpu.CompilerParams(vmem_limit_bytes=VMEM_LIMIT),
        name="finish",
    )(*arrays.values())


def on_device(
    dp,
    hidden_in,
    document_time_vectors,
    segment_ids,
    first_gain,
    first_shift,
    query_weight,
    query_bias,
    key_weight,
    value_weight,
    value_bias,
    out_weight,
    out_bias,
    second_gain,
    second_shift,
    up_weight,
    up_bias,
    down_weight,
    down_bias,
    cotangent,
):
    length, width = hidden_in.shape
    cols, hidden = query_weight.shape[1], up_weight.shape[1]
    s = Shape(length, width, cols, hidden, document_time_vectors.shape[1], dp)

    vectors = dict(
        segments=segment_ids,
        doc_vectors=document_time_vectors,
        first_gain=first_gain,
        first_shift=first_shift,
        second_gain=second_gain,
        second_shift=second_shift,
        out_bias=out_bias,
        down_bias=down_bias,
        up_bias=up_bias,
        query_bias=query_bias,
        value_bias=value_bias,
    )
    arrays = dict(
        hidden=hidden_in,
        cotangent=cotangent,
        query=query_weight.T,
        key=key_weight.T,
        value=value_weight.T,
        out=out_weight,
        up=up_weight,
        down=down_weight,
    )
    layer_out, input_grad, embed, grads, sums = layer_call(s, vectors, arrays)
    if not s.short:
        grads = grads.reshape(3, width, width)
        grads = lax.psum_scatter(grads, "dp", scatter_dimension=1, tiled=True).astype(F32)
        sums = lax.psum(sums, "dp")
    results = finish_call(s, layer_out, input_grad, embed, grads, sums)
    results = [y.reshape(y.shape[1]) if y.ndim == 2 and y.shape[0] == 1 else y for y in results]
    results[16] = results[16].T
    return tuple(results)


def solution(mesh):
    placed = (
        P("dp", None),
        P("dp", None, None),
        P("dp", None),
        P(),
        P(),
        P(None, "tensor"),
        P("tensor"),
        P(None, "tensor"),
        P(None, "tensor"),
        P("tensor"),
        P("tensor", None),
        P(),
        P(),
        P(),
        P(None, "tensor"),
        P("tensor"),
        P("tensor", None),
        P(),
        P("dp", None),
    )
    return jax.shard_map(
        functools.partial(on_device, mesh.shape["dp"]),
        mesh=mesh,
        in_specs=placed,
        out_specs=(
            P("dp", None),
            P("dp", None),
            P("dp", None, None),
            P("dp"),
            P("dp"),
            P("dp", "tensor"),
            P(("tensor", "dp")),
            P("dp", "tensor"),
            P("dp", "tensor"),
            P(("tensor", "dp")),
            P("tensor", "dp"),
            P("dp"),
            P("dp"),
            P("dp"),
            P("dp", "tensor"),
            P(("tensor", "dp")),
            P("tensor", "dp"),
            P("dp"),
        ),
        check_vma=False,
    )
```
